32 devices in a mesh: tm: 4 (over y, core), lat: 4 (over z), lon: 2 (over x).
Axes of the slice: x: 2, y: 2, z: 4, core: 2. Of those that a mesh axis runs over, the one named last changes fastest.
Arguments:
- state: bfloat16 [4, 4, 137, 32, 512], P('tm', None, None, 'lat', 'lon'), may hold values from -6 to 6
- band_counts: int32 [4, 4], P('tm', 'lat'), may hold values from 2 to 6
- dep_blocks: int32 [4, 32, 4, 6], P('tm', 'lat', 'lon'), may hold values from 0 to 3, as said below
- lon_entry: int32 [4, 32, 512], P('tm', 'lat', 'lon'), may hold values from 0 to 5
- lon_offset: int32 [4, 32, 512], P('tm', 'lat', 'lon'), may hold values from 1 to 125
- lon_frac: float32 [4, 32, 512], P('tm', 'lat', 'lon'), may hold values from 0 to 1
- lat_offset: int32 [4, 32, 512], P('tm', 'lat', 'lon'), may hold values from -1 to 0
- lat_frac: float32 [4, 32, 512], P('tm', 'lat', 'lon'), may hold values from 0 to 1
Outputs:
- misfit: bfloat16 [4, 4, 137, 32, 512], P('tm', None, None, 'lat', 'lon')
The draws below stay inside these ranges and needn't reach their ends.
Inputs may be any that keep to these rules, and one draw needn't show every extreme that they name: `dep_blocks`: the list of a destination block names each of the 6 blocks of its latitude row that lie from 3 blocks west of the first block of the destination's tile to 1 block east of the tile's last block (block numbers taken modulo 4) exactly once, in an order drawn for each block.
All inputs are finite; a program needn't handle non-finite values.
Results may differ from the reference program's by a relative error of at most 0.0046.
Values may be sent and summed in bfloat16 or wider, within the bound.
A program may use at most 64 MiB of HBM per device.

```python
import jax
import jax.numpy as jnp
from jax import lax

VARS = 4
LEV = 137
BLK = 128
NB = 2
RL = 8
KMAX = 6
WINDOWS = 4
BANDS = 4
NROWS = 32
CYCLE = 4
COLS = 512


def draw_dep_blocks(key, part):
    keyed = jax.random.fold_in(jax.random.fold_in(key, 202), part)
    scores = jax.random.randint(jax.random.fold_in(keyed, 21), (WINDOWS, NROWS, CYCLE, KMAX), 0, 2 ** 20, dtype=jnp.int32)
    scores = scores * KMAX + jnp.arange(KMAX, dtype=jnp.int32)
    ordering = jnp.argsort(scores, axis=-1, stable=True).astype(jnp.int32)
    block_index = jnp.arange(CYCLE, dtype=jnp.int32)
    tile_start = block_index // NB * NB
    return ((tile_start[None, None, :, None] - NB - NB // 2 + ordering) % CYCLE).astype(jnp.int32)


def place_ends(entries, key, smallest, top_value):
    place = [jax.random.randint(jax.random.fold_in(key, axis), (), 0, length) for axis, length in enumerate(entries.shape)]
    longest = entries.shape.index(max(entries.shape))
    neighbour = place[:longest] + [(place[longest] + 1) % entries.shape[longest]] + place[longest + 1:]
    return entries.at[tuple(place)].set(smallest).at[tuple(neighbour)].set(top_value)


def block_scale(stream_key, shape, split, least, top_value):
    level, own = 1.0, jax.random.fold_in(stream_key, 6)
    for dim, parts in split:
        heights = jnp.exp(jax.random.uniform(jax.random.fold_in(own, dim), (parts,), jnp.float32, least / len(split), top_value / len(split)))
        level = level * jnp.repeat(heights, shape[dim] // parts).reshape([-1 if axis == dim else 1 for axis in range(len(shape))])
    return level


def gaussian(rng, dims, spread, bound, cuts=(), kind=jnp.bfloat16):
    factor_of = block_scale(rng, dims, cuts, -0.22, 0.18) if cuts else 1.0
    result = jax.random.normal(rng, dims, jnp.float32) * spread * factor_of
    return jnp.minimum(jnp.maximum(result, -bound), bound).astype(kind)


def setup_inputs(seed: int = 0) -> dict:
    splits = jax.random.split(jax.random.key(seed), 9)
    state = gaussian(splits[0], (WINDOWS, VARS, LEV, NROWS, COLS), 1.0, 6.0, ((0, 4), (3, 4), (4, 2)))
    band_counts = place_ends(jax.random.randint(splits[1], (WINDOWS, BANDS), 2, KMAX + 1), jax.random.fold_in(splits[1], 1), 2, KMAX).astype(jnp.int32)
    dep_blocks = draw_dep_blocks(jax.random.fold_in(splits[8], 71), 0)
    lon_entry = place_ends(jax.random.randint(splits[3], (WINDOWS, NROWS, COLS), 0, KMAX), jax.random.fold_in(splits[3], 1), 0, KMAX - 1).astype(jnp.int32)
    lon_offset = place_ends(jax.random.randint(splits[4], (WINDOWS, NROWS, COLS), 1, BLK - 2), jax.random.fold_in(splits[4], 1), 1, (BLK - 2) - 1).astype(jnp.int32)
    lon_frac = jnp.clip(1.0 * jax.random.uniform(splits[5], (WINDOWS, NROWS, COLS), jnp.float32) ** block_scale(splits[5], (WINDOWS, NROWS, COLS), ((0, 4), (1, 4), (2, 2)), -0.2, 0.2), 0.0, 1.0)
    lat_offset = place_ends(jax.random.randint(splits[6], (WINDOWS, NROWS, COLS), -1, 1), jax.random.fold_in(splits[6], 1), -1, 0).astype(jnp.int32)
    lat_frac = jnp.clip(1.0 * jax.random.uniform(splits[7], (WINDOWS, NROWS, COLS), jnp.float32) ** block_scale(splits[7], (WINDOWS, NROWS, COLS), ((0, 4), (1, 4), (2, 2)), -0.2, 0.2), 0.0, 1.0)
    return {"state": state, "band_counts": band_counts, "dep_blocks": dep_blocks, "lon_entry": lon_entry, "lon_offset": lon_offset, "lon_frac": lon_frac, "lat_offset": lat_offset, "lat_frac": lat_frac}


def cubic_weights(fraction):
    return jnp.stack([
        -fraction * (fraction - 1.0) * (fraction - 2.0) / 6.0,
        (fraction + 1.0) * (fraction - 1.0) * (fraction - 2.0) / 2.0,
        -(fraction + 1.0) * fraction * (fraction - 2.0) / 2.0,
        (fraction + 1.0) * fraction * (fraction - 1.0) / 6.0,
    ])


def reference(state, band_counts, dep_blocks, lon_entry, lon_offset, lon_frac, lat_offset, lat_frac):
    depth_rows = VARS * LEV
    windows = state.reshape(WINDOWS, depth_rows, NROWS, COLS)
    band_of_row = jnp.arange(NROWS, dtype=jnp.int32) // RL
    block_of_col = jnp.arange(COLS, dtype=jnp.int32) // BLK
    stencil_nodes = jnp.arange(4, dtype=jnp.int32)

    def one_window(previous, window):
        fields, counts, departure_lists, entry_rows, offset_rows, fraction_rows, lat_shift, lat_fraction = window
        by_row = jnp.swapaxes(fields, 0, 1)

        def one_row(row_data):
            source_row, list_row, entry_row, offset_row, fraction_row, band_index = row_data
            entry_slot = entry_row % counts[band_index]
            chosen = jnp.take_along_axis(list_row[block_of_col], entry_slot[:, None], axis=1)[:, 0]
            positions = (chosen[:, None] * BLK + offset_row[:, None] - 1 + stencil_nodes[None, :]).astype(jnp.int32)
            rounded = lax.optimization_barrier(cubic_weights(fraction_row).astype(jnp.bfloat16))
            weights = rounded.astype(jnp.float32)
            picked = source_row[:, positions].astype(jnp.float32)
            return jnp.sum(picked * weights.T[None, :, :], axis=2).astype(jnp.bfloat16)

        advected = lax.map(one_row, (by_row, departure_lists, entry_rows, offset_rows, fraction_rows, band_of_row))
        padded = jnp.pad(advected, ((2, 2), (0, 0), (0, 0)))
        lat_weights = cubic_weights(lat_fraction)
        end_sum = jnp.zeros((NROWS, depth_rows, COLS), jnp.float32)
        for shift_rows in range(-2, 3):
            coefficient = jnp.zeros((NROWS, COLS), jnp.float32)
            for node_index in range(4):
                coefficient = coefficient + jnp.where(lat_shift + node_index - 1 == shift_rows, lat_weights[node_index], 0.0)
            end_sum = end_sum + coefficient[:, None, :] * padded[2 + shift_rows:2 + shift_rows + NROWS].astype(jnp.float32)
        end_state = end_sum.astype(jnp.bfloat16)
        misfit_rows = (by_row.astype(jnp.float32) - previous.astype(jnp.float32)).astype(jnp.bfloat16)
        return end_state, misfit_rows

    start = jnp.zeros((NROWS, depth_rows, COLS), jnp.bfloat16)
    _, misfits = lax.scan(one_window, start, (windows, band_counts, dep_blocks, lon_entry, lon_offset, lon_frac, lat_offset, lat_frac))
    return jnp.swapaxes(misfits, 1, 2).reshape(WINDOWS, VARS, LEV, NROWS, COLS)
```

```python
import functools

import jax
import jax.numpy as jnp
from jax import lax
from jax.experimental import pallas as pl
from jax.experimental.pallas import tpu as pltpu
from jax.sharding import PartitionSpec as P

BLK = 128
CHUNK = 56
MESH = pl.DeviceIdType.MESH


def cubic_weights(fraction):
    return jnp.stack(
        [
            -fraction * (fraction - 1.0) * (fraction - 2.0) / 6.0,
            (fraction + 1.0) * (fraction - 1.0) * (fraction - 2.0) / 2.0,
            -(fraction + 1.0) * fraction * (fraction - 2.0) / 2.0,
            (fraction + 1.0) * fraction * (fraction - 1.0) / 6.0,
        ]
    )


def source_plan(blocks, devices):
    spread = blocks + blocks // 2
    count = min(3 * blocks, blocks * devices)
    slots, pieces, at = [None] * count, [], blocks
    for q in range(count):
        offset, block = divmod(q - spread, blocks)
        if offset % devices == 0:
            slots[q] = block
            continue
        if pieces and pieces[-1][0] == offset and pieces[-1][1] + pieces[-1][2] == block:
            pieces[-1][2] += 1
        else:
            pieces.append([offset, block, 1, at])
        slots[q] = at
        at += 1
    return slots, [tuple(piece) for piece in pieces], at


def kernel(plan, steps, depth, sizes, state, prm, prev, *scratch):
    _, pieces, n_src = plan
    n_tm, n_lat, n_lon = sizes
    n_pieces = len(pieces)
    own, remotes = scratch[0], scratch[1 : 1 + n_pieces]
    (
        flat, params, matrix, adv, f_end, ends, own_sem, x_send, x_recv,
        h_send, h_recv, t_send, t_recv, raw_send, p_send, p_recv,
    ) = scratch[1 + n_pieces :]
    rows, cols = state.shape[1:]
    tm, lat, lon = lax.axis_index("tm"), lax.axis_index("lat"), lax.axis_index("lon")

    helping = n_tm >= 3
    helper, helped = n_tm - 1, n_tm - 3
    half = steps // 2
    is_helper = tm == helper
    if helping:
        first = jnp.where(is_helper, half, 0)
        last = jnp.where(tm == helped, half, steps)
        target = jnp.where(is_helper, helped + 1, tm + 1)
    else:
        first = 0
        last = jnp.where(is_helper, 0, steps)
        target = tm + 1

    barrier = pltpu.get_barrier_semaphore()
    lon_near = sorted({p[0] % n_lon for p in pieces} | {-p[0] % n_lon for p in pieces})
    greeted = len(lon_near)
    for o in lon_near:
        pl.semaphore_signal(
            barrier, inc=1, device_id={"lon": lax.rem(lon + o, n_lon)}, device_id_type=MESH
        )

    def greet(condition, device):
        @pl.when(condition)
        def _():
            pl.semaphore_signal(barrier, inc=1, device_id=device, device_id_type=MESH)

        return jnp.where(condition, 1, 0)

    greeted += greet(lat > 0, {"lat": lat - 1}) + greet(lat < n_lat - 1, {"lat": lat + 1})
    greeted += greet(tm > 0, {"tm": tm - 1}) + greet(tm < n_tm - 1, {"tm": tm + 1})
    if helping:
        greeted += greet(tm == helped, {"tm": helper}) + greet(is_helper, {"tm": helped})
    pl.semaphore_wait(barrier, greeted)

    def begin(c):
        return jnp.minimum(c * CHUNK, depth - CHUNK)

    def own_copy(c):
        return pltpu.make_async_copy(state.at[pl.ds(begin(c), CHUNK)], own.at[c], own_sem.at[c])

    def raw_copy(c):
        return pltpu.make_async_remote_copy(
            src_ref=state.at[pl.ds(begin(c), CHUNK)], dst_ref=own.at[c], send_sem=raw_send.at[c],
            recv_sem=own_sem.at[c], device_id={"tm": helper}, device_id_type=MESH,
        )

    def prm_copy():
        return pltpu.make_async_remote_copy(
            src_ref=prm, dst_ref=params, send_sem=p_send, recv_sem=p_recv,
            device_id={"tm": helper}, device_id_type=MESH,
        )

    def x_copies(c):
        copies = []
        for i, (offset, block, number, _) in enumerate(pieces):
            copies.append(
                pltpu.make_async_remote_copy(
                    src_ref=own.at[c, :, :, pl.ds(block * BLK, number * BLK)],
                    dst_ref=remotes[i].at[c],
                    send_sem=x_send.at[i, c], recv_sem=x_recv.at[i, c],
                    device_id={"lon": lax.rem(lon - offset + 2 * n_lon, n_lon)},
                    device_id_type=MESH,
                )
            )
        return copies

    def halo_up(c):
        return pltpu.make_async_remote_copy(
            src_ref=adv.at[c, pl.ds(rows, 2)], dst_ref=adv.at[c, pl.ds(0, 2)],
            send_sem=h_send.at[0, c], recv_sem=h_recv.at[0, c],
            device_id={"lat": lat + 1}, device_id_type=MESH,
        )

    def halo_down(c):
        return pltpu.make_async_remote_copy(
            src_ref=adv.at[c, pl.ds(2, 2)], dst_ref=adv.at[c, pl.ds(rows + 2, 2)],
            send_sem=h_send.at[1, c], recv_sem=h_recv.at[1, c],
            device_id={"lat": lat - 1}, device_id_type=MESH,
        )

    rest = depth - (steps - 1) * CHUNK

    def end_copy(c, short):
        if short:
            source, place = ends.at[c, pl.ds(CHUNK - rest, rest)], pl.ds((steps - 1) * CHUNK, rest)
        else:
            source, place = ends.at[c], pl.ds(c * CHUNK, CHUNK)
        return pltpu.make_async_remote_copy(
            src_ref=source, dst_ref=prev.at[place], send_sem=t_send.at[c], recv_sem=t_recv.at[c],
            device_id={"tm": target}, device_id_type=MESH,
        )

    def each_end(c, act):
        @pl.when(c < steps - 1)
        def _():
            act(end_copy(c, False))

        @pl.when(c == steps - 1)
        def _():
            act(end_copy(c, True))

    def loop(low, high, act):
        lax.fori_loop(low, high, lambda c, _: (act(c), 0)[1], 0)

    local = jnp.logical_not(is_helper)

    @pl.when(local)
    def _():
        loop(first, last, lambda c: own_copy(c).start())
        pltpu.make_async_copy(prm, params, p_recv).start()

    if helping:

        @pl.when(tm == helped)
        def _():
            prm_copy().start()
            loop(half, steps, lambda c: raw_copy(c).start())

    def forward(c):
        own_copy(c).wait()
        for copy in x_copies(c):
            copy.start()

    ahead = jnp.where(is_helper, 2, steps)
    loop(first, jnp.minimum(first + ahead, last), forward)

    @pl.when(lat == 0)
    def _():
        adv[:, 0:2] = jnp.zeros((steps, 2, CHUNK, cols), adv.dtype)

    @pl.when(lat == n_lat - 1)
    def _():
        adv[:, rows + 2 : rows + 4] = jnp.zeros((steps, 2, CHUNK, cols), adv.dtype)

    def build(r):
        offset, slot = params[0, pl.ds(r, 1), :], params[1, pl.ds(r, 1), :]
        gap = lax.broadcasted_iota(jnp.int32, (BLK, cols), 0).astype(jnp.float32) - offset
        value = jnp.zeros((BLK, cols), jnp.float32)
        for node in range(4):
            weight = params[2 + node, pl.ds(r, 1), :]
            value = jnp.where(gap == node - 1.0, weight, value)
        for q in range(n_src):
            matrix[r, q * BLK : (q + 1) * BLK, :] = jnp.where(slot == q, value, 0.0).astype(
                jnp.bfloat16
            )

    def advect(c):
        for copy in x_copies(c):
            copy.wait_recv()
        at = 0
        for buffer in (own, *remotes):
            for b in range(buffer.shape[3] // BLK):
                part = buffer[c, :, :, b * BLK : (b + 1) * BLK].astype(jnp.float32)
                flat[at] = part.reshape(CHUNK * rows, BLK)
                at += 1
        for r in [0, 1, rows - 2, rows - 1] + list(range(2, rows - 2)):
            parts = [
                flat[q, pl.ds(r, CHUNK, stride=rows), :].astype(jnp.bfloat16)
                for q in range(n_src)
            ]
            total = jnp.dot(
                jnp.concatenate(parts, axis=1), matrix[r], preferred_element_type=jnp.float32
            )
            adv[c, r + 2] = total.astype(adv.dtype)

        @pl.when(lat < n_lat - 1)
        def _():
            halo_up(c).start()

        @pl.when(lat > 0)
        def _():
            halo_down(c).start()

    def finish(c):
        @pl.when(lat > 0)
        def _():
            halo_up(c).wait_recv()

        @pl.when(lat < n_lat - 1)
        def _():
            halo_down(c).wait_recv()

        for r in range(rows):
            total = None
            for shift in range(5):
                term = params[6 + shift, r : r + 1, :] * adv[c, r + shift].astype(jnp.float32)
                total = term if total is None else total + term
            for b in range(cols // BLK):
                f_end[b, pl.ds(r, CHUNK, stride=rows), :] = total[:, b * BLK : (b + 1) * BLK]
        for b in range(cols // BLK):
            part = f_end[b].reshape(CHUNK, rows, BLK).astype(ends.dtype)
            ends[c, :, :, b * BLK : (b + 1) * BLK] = part
        each_end(c, lambda copy: copy.start())

    def step(c):
        @pl.when(c + ahead < last)
        def _():
            forward(c + ahead)

        @pl.when(c < last)
        def _():
            advect(c)

        @pl.when(c > first)
        def _():
            finish(c - 1)

    def settle(c):
        for copy in x_copies(c):
            copy.wait_send()

        @pl.when(lat < n_lat - 1)
        def _():
            halo_up(c).wait_send()

        @pl.when(lat > 0)
        def _():
            halo_down(c).wait_send()

        each_end(c, lambda copy: copy.wait_send())

    @pl.when(first < last)
    def _():
        pltpu.make_async_copy(prm, params, p_recv).wait()
        loop(0, rows, build)
        loop(first, last + 1, step)
        loop(first, last, settle)

    if helping:

        @pl.when(tm == helped)
        def _():
            prm_copy().wait_send()
            loop(half, steps, lambda c: raw_copy(c).wait_send())

    @pl.when(tm > 0)
    def _():
        loop(0, steps, lambda c: each_end(c, lambda copy: copy.wait_recv()))


def body(sizes, state, band_counts, dep_blocks, lon_entry, lon_offset, lon_frac, lat_offset, lat_frac):
    fields_n, levels, rows, cols = state.shape[1:]
    depth, blocks = fields_n * levels, cols // BLK
    n_tm, n_lat, n_lon = sizes
    plan = source_plan(blocks, n_lon)
    slots, pieces, n_src = plan
    steps = -(-depth // CHUNK)
    flat = state.reshape(depth, rows, cols)

    spread = blocks + blocks // 2
    placed = (dep_blocks[0] - lax.axis_index("lon") * blocks + spread) % (blocks * n_lon)
    slot_of = jnp.zeros_like(placed)
    for q, slot in enumerate(slots):
        slot_of = jnp.where(placed == q, slot, slot_of)
    entry = lon_entry[0] % band_counts[0, 0]
    chosen = jnp.zeros((rows, blocks, BLK), jnp.int32)
    for k in range(dep_blocks.shape[-1]):
        chosen = jnp.where(entry.reshape(rows, blocks, BLK) == k, slot_of[:, :, k : k + 1], chosen)
    chosen = chosen.reshape(rows, cols)
    weights = cubic_weights(lon_frac[0]).astype(jnp.bfloat16).astype(jnp.float32)
    lat_weights = cubic_weights(lat_frac[0])
    coefficients = []
    for shift in range(-2, 3):
        coefficient = jnp.zeros((rows, cols), jnp.float32)
        for node in range(4):
            coefficient = coefficient + jnp.where(
                lat_offset[0] + node - 1 == shift, lat_weights[node], 0.0
            )
        coefficients.append(coefficient)
    prm = jnp.stack(
        [lon_offset[0].astype(jnp.float32), chosen.astype(jnp.float32)]
        + [weights[m] for m in range(4)]
        + coefficients
    )

    dma = pltpu.SemaphoreType.DMA
    n_pieces = len(pieces)
    prev = pl.pallas_call(
        functools.partial(kernel, plan, steps, depth, sizes),
        out_shape=jax.ShapeDtypeStruct(flat.shape, flat.dtype),
        in_specs=[pl.BlockSpec(memory_space=pl.ANY)] * 2,
        out_specs=pl.BlockSpec(memory_space=pl.ANY),
        scratch_shapes=[
            pltpu.VMEM((steps, CHUNK, rows, cols), flat.dtype),
            *[pltpu.VMEM((steps, CHUNK, rows, p[2] * BLK), flat.dtype) for p in pieces],
            pltpu.VMEM((n_src, CHUNK * rows, BLK), jnp.float32),
            pltpu.VMEM(prm.shape, jnp.float32),
            pltpu.VMEM((rows, n_src * BLK, cols), jnp.bfloat16),
            pltpu.VMEM((steps, rows + 4, CHUNK, cols), flat.dtype),
            pltpu.VMEM((blocks, CHUNK * rows, BLK), jnp.float32),
            pltpu.VMEM((steps, CHUNK, rows, cols), flat.dtype),
            dma((steps,)),
            dma((n_pieces, steps)),
            dma((n_pieces, steps)),
            dma((2, steps)),
            dma((2, steps)),
            dma((steps,)),
            dma((steps,)),
            dma((steps,)),
            dma(()),
            dma(()),
        ],
        compiler_params=pltpu.CompilerParams(
            collective_id=0, has_side_effects=True, vmem_limit_bytes=40 * 1024 * 1024
        ),
    )(flat, prm)
    moved = jnp.where(lax.axis_index("tm") > 0, prev.astype(jnp.float32), 0.0)
    misfit = (flat.astype(jnp.float32) - moved).astype(state.dtype)
    return misfit.reshape(state.shape)


def solution(mesh):
    placed = (
        P("tm", None, None, "lat", "lon"),
        P("tm", "lat"),
        P("tm", "lat", "lon", None),
        P("tm", "lat", "lon"),
        P("tm", "lat", "lon"),
        P("tm", "lat", "lon"),
        P("tm", "lat", "lon"),
        P("tm", "lat", "lon"),
    )
    sizes = tuple(mesh.shape[name] for name in ("tm", "lat", "lon"))
    return jax.shard_map(
        functools.partial(body, sizes),
        mesh=mesh,
        in_specs=placed,
        out_specs=P("tm", None, None, "lat", "lon"),
        check_vma=False,
    )
```

```python
import functools

import jax
import jax.numpy as jnp
from jax import lax
from jax.experimental import pallas as pl
from jax.experimental.pallas import tpu as pltpu
from jax.sharding import PartitionSpec as P

BLK = 128
CHUNK = 72
MESH = pl.DeviceIdType.MESH


def cubic_weights(fraction):
    return [
        -fraction * (fraction - 1.0) * (fraction - 2.0) / 6.0,
        (fraction + 1.0) * (fraction - 1.0) * (fraction - 2.0) / 2.0,
        -(fraction + 1.0) * fraction * (fraction - 2.0) / 2.0,
        (fraction + 1.0) * fraction * (fraction - 1.0) / 6.0,
    ]


def source_plan(blocks, devices):
    spread = blocks + blocks // 2
    count = min(3 * blocks, blocks * devices)
    slots, pieces, at = [None] * count, [], blocks
    for q in range(count):
        offset, block = divmod(q - spread, blocks)
        if offset % devices == 0:
            slots[q] = block
            continue
        if pieces and pieces[-1][0] == offset and pieces[-1][1] + pieces[-1][2] == block:
            pieces[-1][2] += 1
        else:
            pieces.append([offset, block, 1, at])
        slots[q] = at
        at += 1
    return slots, [tuple(piece) for piece in pieces], at


def kernel(plan, steps, depth, sizes, state, counts, lists, *rest_refs):
    slots, pieces, n_src = plan
    arrays, prev, scratch = rest_refs[:5], rest_refs[5], rest_refs[6:]
    n_tm, n_lat, n_lon = sizes
    n_pieces = len(pieces)
    own, remotes = scratch[0], scratch[1 : 1 + n_pieces]
    (
        counts_s, lists_s, *arrays_v, flat, params, matrix, adv, f_end, ends, own_sem, x_send, x_recv,
        h_send, h_recv, t_send, t_recv, raw_send, p_send, p_recv, a_sem,
    ) = scratch[1 + n_pieces :]
    rows, cols = state.shape[1:]
    tm, lat, lon = lax.axis_index("tm"), lax.axis_index("lat"), lax.axis_index("lon")

    helping = n_tm >= 3
    helper, helped = n_tm - 1, n_tm - 3
    half = steps // 2
    rest = depth - (steps - 1) * CHUNK
    is_helper = tm == helper
    if helping:
        first = jnp.where(is_helper, half, 0)
        last = jnp.where(tm == helped, half, steps)
        target = jnp.where(is_helper, helped + 1, tm + 1)
    else:
        first = 0
        last = jnp.where(is_helper, 0, steps)
        target = tm + 1

    barrier = pltpu.get_barrier_semaphore()
    lon_near = sorted({p[0] % n_lon for p in pieces} | {-p[0] % n_lon for p in pieces})
    greeted = len(lon_near)
    for o in lon_near:
        pl.semaphore_signal(
            barrier, inc=1, device_id={"lon": lax.rem(lon + o, n_lon)}, device_id_type=MESH
        )

    def greet(condition, device):
        @pl.when(condition)
        def _():
            pl.semaphore_signal(barrier, inc=1, device_id=device, device_id_type=MESH)

        return jnp.where(condition, 1, 0)

    greeted += greet(lat > 0, {"lat": lat - 1}) + greet(lat < n_lat - 1, {"lat": lat + 1})
    greeted += greet(tm > 0, {"tm": tm - 1}) + greet(tm < n_tm - 1, {"tm": tm + 1})
    if helping:
        greeted += greet(tm == helped, {"tm": helper}) + greet(is_helper, {"tm": helped})
    pl.semaphore_wait(barrier, greeted)

    def begin(c):
        return jnp.minimum(c * CHUNK, depth - CHUNK)

    def own_copy(c):
        return pltpu.make_async_copy(state.at[pl.ds(begin(c), CHUNK)], own.at[c], own_sem.at[c])

    def raw_copy(c):
        return pltpu.make_async_remote_copy(
            src_ref=state.at[pl.ds(begin(c), CHUNK)], dst_ref=own.at[c], send_sem=raw_send.at[c],
            recv_sem=own_sem.at[c], device_id={"tm": helper}, device_id_type=MESH,
        )

    def prm_copy():
        return pltpu.make_async_remote_copy(
            src_ref=params, dst_ref=params, send_sem=p_send, recv_sem=p_recv,
            device_id={"tm": helper}, device_id_type=MESH,
        )

    def x_copies(c, short):
        part = pl.ds(CHUNK - rest, rest) if short else pl.ds(0, CHUNK)
        copies = []
        for i, (offset, block, number, _) in enumerate(pieces):
            copies.append(
                pltpu.make_async_remote_copy(
                    src_ref=own.at[c, part, :, pl.ds(block * BLK, number * BLK)],
                    dst_ref=remotes[i].at[c, part],
                    send_sem=x_send.at[i, c], recv_sem=x_recv.at[i, c],
                    device_id={"lon": lax.rem(lon - offset + 2 * n_lon, n_lon)},
                    device_id_type=MESH,
                )
            )
        return copies

    def each_x(c, act):
        @pl.when(c < steps - 1)
        def _():
            for copy in x_copies(c, False):
                act(copy)

        @pl.when(c == steps - 1)
        def _():
            for copy in x_copies(c, True):
                act(copy)

    def halo_up(c):
        return pltpu.make_async_remote_copy(
            src_ref=adv.at[c, pl.ds(rows, 2)], dst_ref=adv.at[c, pl.ds(0, 2)],
            send_sem=h_send.at[0, c], recv_sem=h_recv.at[0, c],
            device_id={"lat": lat + 1}, device_id_type=MESH,
        )

    def halo_down(c):
        return pltpu.make_async_remote_copy(
            src_ref=adv.at[c, pl.ds(2, 2)], dst_ref=adv.at[c, pl.ds(rows + 2, 2)],
            send_sem=h_send.at[1, c], recv_sem=h_recv.at[1, c],
            device_id={"lat": lat - 1}, device_id_type=MESH,
        )

    def end_copy(c, short):
        if short:
            source, place = ends.at[c, pl.ds(CHUNK - rest, rest)], pl.ds((steps - 1) * CHUNK, rest)
        else:
            source, place = ends.at[c], pl.ds(c * CHUNK, CHUNK)
        return pltpu.make_async_remote_copy(
            src_ref=source, dst_ref=prev.at[place], send_sem=t_send.at[c], recv_sem=t_recv.at[c],
            device_id={"tm": target}, device_id_type=MESH,
        )

    def each_end(c, act):
        @pl.when(c < steps - 1)
        def _():
            act(end_copy(c, False))

        @pl.when(c == steps - 1)
        def _():
            act(end_copy(c, True))

    def loop(low, high, act):
        lax.fori_loop(low, high, lambda c, _: (act(c), 0)[1], 0)

    aux = [
        pltpu.make_async_copy(source, place, a_sem.at[i])
        for i, (source, place) in enumerate(
            [(counts, counts_s), (lists, lists_s)]
            + [(array.at[0], place) for array, place in zip(arrays, arrays_v)]
        )
    ]
    local = jnp.logical_not(is_helper)

    @pl.when(local)
    def _():
        loop(first, last, lambda c: own_copy(c).start())
        for copy in aux:
            copy.start()

    if helping:

        @pl.when(tm == helped)
        def _():
            loop(half, steps, lambda c: raw_copy(c).start())

    def forward(c):
        own_copy(c).wait()
        each_x(c, lambda copy: copy.start())

    ahead = jnp.where(is_helper, 2, steps)
    loop(first, jnp.minimum(first + ahead, last), forward)

    @pl.when(lat == 0)
    def _():
        adv[:, 0:2] = jnp.zeros((steps, 2, CHUNK, cols), adv.dtype)

    @pl.when(lat == n_lat - 1)
    def _():
        adv[:, rows + 2 : rows + 4] = jnp.zeros((steps, 2, CHUNK, cols), adv.dtype)

    def prepare():
        for copy in aux:
            copy.wait()
        entry, offset, lon_fraction, lat_shift, lat_fraction = [v[...] for v in arrays_v]
        per_list = lists.shape[-1]
        for _ in range((per_list - 1) // 2):
            entry = jnp.where(entry >= counts_s[0, 0], entry - counts_s[0, 0], entry)
        blocks = cols // BLK
        total = blocks * n_lon
        for r in range(rows):
            for g in range(blocks):
                wanted = entry[r : r + 1, g * BLK : (g + 1) * BLK]
                chosen = jnp.zeros((1, BLK), jnp.int32)
                for k in range(per_list):
                    q = lists_s[0, r, g, k] - lon * blocks + blocks + blocks // 2 + total
                    q = lax.rem(q, total)
                    slot = jnp.int32(slots[0])
                    for i in range(1, len(slots)):
                        slot = jnp.where(q == i, slots[i], slot)
                    chosen = jnp.where(wanted == k, slot, chosen)
                params[1, r : r + 1, g * BLK : (g + 1) * BLK] = chosen.astype(jnp.float32)
        params[0] = offset.astype(jnp.float32)
        for node, weight in enumerate(cubic_weights(lon_fraction)):
            params[2 + node] = weight.astype(jnp.bfloat16).astype(jnp.float32)
        lat_weights = cubic_weights(lat_fraction)
        for shift in range(-2, 3):
            coefficient = jnp.zeros((rows, cols), jnp.float32)
            for node in range(4):
                coefficient = coefficient + jnp.where(
                    lat_shift + node - 1 == shift, lat_weights[node], 0.0
                )
            params[8 + shift] = coefficient

    def build(r):
        offset, slot = params[0, pl.ds(r, 1), :], params[1, pl.ds(r, 1), :]
        gap = lax.broadcasted_iota(jnp.int32, (BLK, cols), 0).astype(jnp.float32) - offset
        value = jnp.zeros((BLK, cols), jnp.float32)
        for node in range(4):
            weight = params[2 + node, pl.ds(r, 1), :]
            value = jnp.where(gap == node - 1.0, weight, value)
        for q in range(n_src):
            matrix[r, q * BLK : (q + 1) * BLK, :] = jnp.where(slot == q, value, 0.0).astype(
                jnp.bfloat16
            )

    def advect(c):
        each_x(c, lambda copy: copy.wait_recv())
        at = 0
        for buffer in (own, *remotes):
            for b in range(buffer.shape[3] // BLK):
                part = buffer[c, :, :, b * BLK : (b + 1) * BLK].astype(jnp.float32)
                flat[at] = part.reshape(CHUNK * rows, BLK)
                at += 1
        for r in [0, 1, rows - 2, rows - 1] + list(range(2, rows - 2)):
            parts = [
                flat[q, pl.ds(r, CHUNK, stride=rows), :].astype(jnp.bfloat16)
                for q in range(n_src)
            ]
            total = jnp.dot(
                jnp.concatenate(parts, axis=1), matrix[r], preferred_element_type=jnp.float32
            )
            adv[c, r + 2] = total.astype(adv.dtype)

        @pl.when(lat < n_lat - 1)
        def _():
            halo_up(c).start()

        @pl.when(lat > 0)
        def _():
            halo_down(c).start()

    def finish(c):
        @pl.when(lat > 0)
        def _():
            halo_up(c).wait_recv()

        @pl.when(lat < n_lat - 1)
        def _():
            halo_down(c).wait_recv()

        for r in range(rows):
            total = None
            for shift in range(5):
                term = params[6 + shift, r : r + 1, :] * adv[c, r + shift].astype(jnp.float32)
                total = term if total is None else total + term
            for b in range(cols // BLK):
                f_end[b, pl.ds(r, CHUNK, stride=rows), :] = total[:, b * BLK : (b + 1) * BLK]
        for b in range(cols // BLK):
            part = f_end[b].reshape(CHUNK, rows, BLK).astype(ends.dtype)
            ends[c, :, :, b * BLK : (b + 1) * BLK] = part
        each_end(c, lambda copy: copy.start())

    def step(c):
        @pl.when(c + ahead < last)
        def _():
            forward(c + ahead)

        @pl.when(c < last)
        def _():
            advect(c)

        @pl.when(c > first)
        def _():
            finish(c - 1)

    def settle(c):
        each_x(c, lambda copy: copy.wait_send())

        @pl.when(lat < n_lat - 1)
        def _():
            halo_up(c).wait_send()

        @pl.when(lat > 0)
        def _():
            halo_down(c).wait_send()

        each_end(c, lambda copy: copy.wait_send())

    @pl.when(first < last)
    def _():
        pl.when(local)(prepare)
        if helping:

            @pl.when(tm == helped)
            def _():
                prm_copy().start()

            @pl.when(is_helper)
            def _():
                prm_copy().wait_recv()

        loop(0, rows, build)
        loop(first, last + 1, step)
        loop(first, last, settle)

    if helping:

        @pl.when(tm == helped)
        def _():
            prm_copy().wait_send()
            loop(half, steps, lambda c: raw_copy(c).wait_send())

    @pl.when(tm > 0)
    def _():
        loop(0, steps, lambda c: each_end(c, lambda copy: copy.wait_recv()))


def body(sizes, state, band_counts, dep_blocks, lon_entry, lon_offset, lon_frac, lat_offset, lat_frac):
    fields_n, levels, rows, cols = state.shape[1:]
    depth, blocks = fields_n * levels, cols // BLK
    n_tm, n_lat, n_lon = sizes
    plan = source_plan(blocks, n_lon)
    _, pieces, n_src = plan
    steps = -(-depth // CHUNK)
    flat = state.reshape(depth, rows, cols)

    dma = pltpu.SemaphoreType.DMA
    n_pieces = len(pieces)
    prev = pl.pallas_call(
        functools.partial(kernel, plan, steps, depth, sizes),
        out_shape=jax.ShapeDtypeStruct(flat.shape, flat.dtype),
        in_specs=[pl.BlockSpec(memory_space=pltpu.HBM)] * 8,
        out_specs=pl.BlockSpec(memory_space=pl.ANY),
        scratch_shapes=[
            pltpu.VMEM((steps, CHUNK, rows, cols), flat.dtype),
            *[pltpu.VMEM((steps, CHUNK, rows, p[2] * BLK), flat.dtype) for p in pieces],
            pltpu.SMEM(band_counts.shape, jnp.int32),
            pltpu.SMEM(dep_blocks.shape, jnp.int32),
            *[
                pltpu.VMEM((rows, cols), kind.dtype)
                for kind in (lon_entry, lon_offset, lon_frac, lat_offset, lat_frac)
            ],
            pltpu.VMEM((n_src, CHUNK * rows, BLK), jnp.float32),
            pltpu.VMEM((11, rows, cols), jnp.float32),
            pltpu.VMEM((rows, n_src * BLK, cols), jnp.bfloat16),
            pltpu.VMEM((steps, rows + 4, CHUNK, cols), flat.dtype),
            pltpu.VMEM((blocks, CHUNK * rows, BLK), jnp.float32),
            pltpu.VMEM((steps, CHUNK, rows, cols), flat.dtype),
            dma((steps,)),
            dma((n_pieces, steps)),
            dma((n_pieces, steps)),
            dma((2, steps)),
            dma((2, steps)),
            dma((steps,)),
            dma((steps,)),
            dma((steps,)),
            dma(()),
            dma(()),
            dma((7,)),
        ],
        compiler_params=pltpu.CompilerParams(
            collective_id=0, has_side_effects=True, vmem_limit_bytes=40 * 1024 * 1024
        ),
    )(flat, band_counts, dep_blocks, lon_entry, lon_offset, lon_frac, lat_offset, lat_frac)
    moved = jnp.where(lax.axis_index("tm") > 0, prev.astype(jnp.float32), 0.0)
    misfit = (flat.astype(jnp.float32) - moved).astype(state.dtype)
    return misfit.reshape(state.shape)


def solution(mesh):
    placed = (
        P("tm", None, None, "lat", "lon"),
        P("tm", "lat"),
        P("tm", "lat", "lon", None),
        P("tm", "lat", "lon"),
        P("tm", "lat", "lon"),
        P("tm", "lat", "lon"),
        P("tm", "lat", "lon"),
        P("tm", "lat", "lon"),
    )
    sizes = tuple(mesh.shape[name] for name in ("tm", "lat", "lon"))
    return jax.shard_map(
        functools.partial(body, sizes),
        mesh=mesh,
        in_specs=placed,
        out_specs=P("tm", None, None, "lat", "lon"),
        check_vma=False,
    )
```

```python
import functools

import jax
import jax.numpy as jnp
from jax import lax
from jax.experimental import pallas as pl
from jax.experimental.pallas import tpu as pltpu
from jax.sharding import PartitionSpec as P

BLK = 128
CHUNK = 72
MESH = pl.DeviceIdType.MESH


def cubic_weights(fraction):
    return [
        -fraction * (fraction - 1.0) * (fraction - 2.0) / 6.0,
        (fraction + 1.0) * (fraction - 1.0) * (fraction - 2.0) / 2.0,
        -(fraction + 1.0) * fraction * (fraction - 2.0) / 2.0,
        (fraction + 1.0) * fraction * (fraction - 1.0) / 6.0,
    ]


def source_plan(blocks, devices):
    spread = blocks + blocks // 2
    count = min(3 * blocks, blocks * devices)
    slots, pieces, at = [None] * count, [], blocks
    for q in range(count):
        offset, block = divmod(q - spread, blocks)
        if offset % devices == 0:
            slots[q] = block
            continue
        if pieces and pieces[-1][0] == offset and pieces[-1][1] + pieces[-1][2] == block:
            pieces[-1][2] += 1
        else:
            pieces.append([offset, block, 1, at])
        slots[q] = at
        at += 1
    return slots, [tuple(piece) for piece in pieces], at


def kernel(plan, steps, depth, sizes, state, counts, lists, *rest_refs):
    slots, pieces, n_src = plan
    arrays, prev, scratch = rest_refs[:5], rest_refs[5], rest_refs[6:]
    n_tm, n_lat, n_lon = sizes
    n_pieces = len(pieces)
    own, remotes = scratch[0], scratch[1 : 1 + n_pieces]
    (
        counts_s, lists_s, *arrays_v, flat, params, matrix, adv, f_end, ends, own_sem, x_send, x_recv,
        h_send, h_recv, t_send, t_recv, raw_send, p_send, p_recv, a_sem,
    ) = scratch[1 + n_pieces :]
    rows, cols = state.shape[1:]
    tm, lat, lon = lax.axis_index("tm"), lax.axis_index("lat"), lax.axis_index("lon")

    helping = n_tm >= 3
    helper, helped = n_tm - 1, n_tm - 3
    half = steps // 2
    rest = depth - (steps - 1) * CHUNK
    is_helper = tm == helper
    if helping:
        first = jnp.where(is_helper, half, 0)
        last = jnp.where(tm == helped, half, steps)
        target = jnp.where(is_helper, helped + 1, tm + 1)
    else:
        first = 0
        last = jnp.where(is_helper, 0, steps)
        target = tm + 1

    barrier = pltpu.get_barrier_semaphore()
    lon_near = sorted({p[0] % n_lon for p in pieces} | {-p[0] % n_lon for p in pieces})
    greeted = len(lon_near)
    for o in lon_near:
        pl.semaphore_signal(
            barrier, inc=1, device_id={"lon": lax.rem(lon + o, n_lon)}, device_id_type=MESH
        )

    def greet(condition, device):
        @pl.when(condition)
        def _():
            pl.semaphore_signal(barrier, inc=1, device_id=device, device_id_type=MESH)

        return jnp.where(condition, 1, 0)

    greeted += greet(lat > 0, {"lat": lat - 1}) + greet(lat < n_lat - 1, {"lat": lat + 1})
    greeted += greet(tm > 0, {"tm": tm - 1}) + greet(tm < n_tm - 1, {"tm": tm + 1})
    if helping:
        greeted += greet(tm == helped, {"tm": helper}) + greet(is_helper, {"tm": helped})
    pl.semaphore_wait(barrier, greeted)

    def begin(c):
        return jnp.minimum(c * CHUNK, depth - CHUNK)

    def own_copy(c):
        return pltpu.make_async_copy(state.at[pl.ds(begin(c), CHUNK)], own.at[c], own_sem.at[c])

    def raw_copy(c):
        return pltpu.make_async_remote_copy(
            src_ref=state.at[pl.ds(begin(c), CHUNK)], dst_ref=own.at[c], send_sem=raw_send.at[c],
            recv_sem=own_sem.at[c], device_id={"tm": helper}, device_id_type=MESH,
        )

    def prm_copy():
        return pltpu.make_async_remote_copy(
            src_ref=params, dst_ref=params, send_sem=p_send, recv_sem=p_recv,
            device_id={"tm": helper}, device_id_type=MESH,
        )

    def x_copies(c, short):
        part = pl.ds(CHUNK - rest, rest) if short else pl.ds(0, CHUNK)
        copies = []
        for i, (offset, block, number, _) in enumerate(pieces):
            copies.append(
                pltpu.make_async_remote_copy(
                    src_ref=own.at[c, part, :, pl.ds(block * BLK, number * BLK)],
                    dst_ref=remotes[i].at[c, part],
                    send_sem=x_send.at[i, c], recv_sem=x_recv.at[i, c],
                    device_id={"lon": lax.rem(lon - offset + 2 * n_lon, n_lon)},
                    device_id_type=MESH,
                )
            )
        return copies

    def each_x(c, act):
        @pl.when(c < steps - 1)
        def _():
            for copy in x_copies(c, False):
                act(copy)

        @pl.when(c == steps - 1)
        def _():
            for copy in x_copies(c, True):
                act(copy)

    def halo_up(c):
        return pltpu.make_async_remote_copy(
            src_ref=adv.at[c, pl.ds(rows, 2)], dst_ref=adv.at[c, pl.ds(0, 2)],
            send_sem=h_send.at[0, c], recv_sem=h_recv.at[0, c],
            device_id={"lat": lat + 1}, device_id_type=MESH,
        )

    def halo_down(c):
        return pltpu.make_async_remote_copy(
            src_ref=adv.at[c, pl.ds(2, 2)], dst_ref=adv.at[c, pl.ds(rows + 2, 2)],
            send_sem=h_send.at[1, c], recv_sem=h_recv.at[1, c],
            device_id={"lat": lat - 1}, device_id_type=MESH,
        )

    def end_copy(c, short):
        if short:
            source, place = ends.at[c, pl.ds(CHUNK - rest, rest)], pl.ds((steps - 1) * CHUNK, rest)
        else:
            source, place = ends.at[c], pl.ds(c * CHUNK, CHUNK)
        return pltpu.make_async_remote_copy(
            src_ref=source, dst_ref=prev.at[place], send_sem=t_send.at[c], recv_sem=t_recv.at[c],
            device_id={"tm": target}, device_id_type=MESH,
        )

    def each_end(c, act):
        @pl.when(c < steps - 1)
        def _():
            act(end_copy(c, False))

        @pl.when(c == steps - 1)
        def _():
            act(end_copy(c, True))

    def loop(low, high, act):
        lax.fori_loop(low, high, lambda c, _: (act(c), 0)[1], 0)

    aux = [
        pltpu.make_async_copy(source, place, a_sem.at[i])
        for i, (source, place) in enumerate(
            [(counts, counts_s), (lists, lists_s)]
            + [(array.at[0], place) for array, place in zip(arrays, arrays_v)]
        )
    ]
    local = jnp.logical_not(is_helper)

    @pl.when(local)
    def _():
        loop(first, last, lambda c: own_copy(c).start())
        for copy in aux:
            copy.start()

    if helping:

        @pl.when(tm == helped)
        def _():
            loop(half, steps, lambda c: raw_copy(c).start())

    def forward(c):
        own_copy(c).wait()
        each_x(c, lambda copy: copy.start())

    ahead = jnp.where(is_helper, 2, steps)
    loop(first, jnp.minimum(first + ahead, last), forward)

    @pl.when(lat == 0)
    def _():
        adv[:, 0:2] = jnp.zeros((steps, 2, CHUNK, cols), adv.dtype)

    @pl.when(lat == n_lat - 1)
    def _():
        adv[:, rows + 2 : rows + 4] = jnp.zeros((steps, 2, CHUNK, cols), adv.dtype)

    def prepare():
        for copy in aux:
            copy.wait()
        entry, offset, lon_fraction, lat_shift, lat_fraction = [v[...] for v in arrays_v]
        per_list = lists.shape[-1]
        for _ in range((per_list - 1) // 2):
            entry = jnp.where(entry >= counts_s[0, 0], entry - counts_s[0, 0], entry)
        blocks = cols // BLK
        total = blocks * n_lon
        for r in range(rows):
            for g in range(blocks):
                wanted = entry[r : r + 1, g * BLK : (g + 1) * BLK]
                chosen = jnp.zeros((1, BLK), jnp.int32)
                for k in range(per_list):
                    q = lists_s[0, r, g, k] - lon * blocks + blocks + blocks // 2 + total
                    q = lax.rem(q, total)
                    slot = jnp.int32(slots[0])
                    for i in range(1, len(slots)):
                        slot = jnp.where(q == i, slots[i], slot)
                    chosen = jnp.where(wanted == k, slot, chosen)
                params[1, r : r + 1, g * BLK : (g + 1) * BLK] = chosen.astype(jnp.float32)
        params[0] = offset.astype(jnp.float32)
        for node, weight in enumerate(cubic_weights(lon_fraction)):
            params[2 + node] = weight.astype(jnp.bfloat16).astype(jnp.float32)
        lat_weights = cubic_weights(lat_fraction)
        for shift in range(-2, 3):
            coefficient = jnp.zeros((rows, cols), jnp.float32)
            for node in range(4):
                coefficient = coefficient + jnp.where(
                    lat_shift + node - 1 == shift, lat_weights[node], 0.0
                )
            params[8 + shift] = coefficient

    def build(r):
        offset, slot = params[0, pl.ds(r, 1), :], params[1, pl.ds(r, 1), :]
        gap = lax.broadcasted_iota(jnp.int32, (BLK, cols), 0).astype(jnp.float32) - offset
        value = jnp.zeros((BLK, cols), jnp.float32)
        for node in range(4):
            weight = params[2 + node, pl.ds(r, 1), :]
            value = jnp.where(gap == node - 1.0, weight, value)
        for q in range(n_src):
            matrix[r, q * BLK : (q + 1) * BLK, :] = jnp.where(slot == q, value, 0.0).astype(
                jnp.bfloat16
            )

    def advect(c):
        each_x(c, lambda copy: copy.wait_recv())
        at = 0
        for buffer in (own, *remotes):
            for b in range(buffer.shape[3] // BLK):
                part = buffer[c, :, :, b * BLK : (b + 1) * BLK].astype(jnp.float32)
                flat[at] = part.reshape(CHUNK * rows, BLK)
                at += 1
        for r in [0, 1, rows - 2, rows - 1] + list(range(2, rows - 2)):
            parts = [
                flat[q, pl.ds(r, CHUNK, stride=rows), :].astype(jnp.bfloat16)
                for q in range(n_src)
            ]
            total = jnp.dot(
                jnp.concatenate(parts, axis=1), matrix[r], preferred_element_type=jnp.float32
            )
            adv[c, r + 2] = total.astype(adv.dtype)

        @pl.when(lat < n_lat - 1)
        def _():
            halo_up(c).start()

        @pl.when(lat > 0)
        def _():
            halo_down(c).start()

    def finish(c):
        @pl.when(lat > 0)
        def _():
            halo_up(c).wait_recv()

        @pl.when(lat < n_lat - 1)
        def _():
            halo_down(c).wait_recv()

        for r in range(rows):
            total = None
            for shift in range(5):
                term = params[6 + shift, r : r + 1, :] * adv[c, r + shift].astype(jnp.float32)
                total = term if total is None else total + term
            for b in range(cols // BLK):
                f_end[b, pl.ds(r, CHUNK, stride=rows), :] = total[:, b * BLK : (b + 1) * BLK]
        for b in range(cols // BLK):
            part = f_end[b].reshape(CHUNK, rows, BLK).astype(ends.dtype)
            ends[c, :, :, b * BLK : (b + 1) * BLK] = part
        each_end(c, lambda copy: copy.start())

    def step(c):
        @pl.when(c + ahead < last)
        def _():
            forward(c + ahead)

        @pl.when(c < last)
        def _():
            advect(c)

        @pl.when(c > first)
        def _():
            finish(c - 1)

    def settle(c):
        each_x(c, lambda copy: copy.wait_send())

        @pl.when(lat < n_lat - 1)
        def _():
            halo_up(c).wait_send()

        @pl.when(lat > 0)
        def _():
            halo_down(c).wait_send()

        each_end(c, lambda copy: copy.wait_send())

    @pl.when(first < last)
    def _():
        pl.when(local)(prepare)
        if helping:

            @pl.when(tm == helped)
            def _():
                prm_copy().start()

            @pl.when(is_helper)
            def _():
                prm_copy().wait_recv()

        loop(0, rows, build)
        loop(first, last + 1, step)
        loop(first, last, settle)

    if helping:

        @pl.when(tm == helped)
        def _():
            prm_copy().wait_send()
            loop(half, steps, lambda c: raw_copy(c).wait_send())

    @pl.when(tm > 0)
    def _():
        loop(0, steps, lambda c: each_end(c, lambda copy: copy.wait_recv()))


def body(sizes, state, band_counts, dep_blocks, lon_entry, lon_offset, lon_frac, lat_offset, lat_frac):
    fields_n, levels, rows, cols = state.shape[1:]
    depth, blocks = fields_n * levels, cols // BLK
    n_tm, n_lat, n_lon = sizes
    plan = source_plan(blocks, n_lon)
    _, pieces, n_src = plan
    steps = -(-depth // CHUNK)
    flat = state.reshape(depth, rows, cols)

    dma = pltpu.SemaphoreType.DMA
    n_pieces = len(pieces)
    prev = pl.pallas_call(
        functools.partial(kernel, plan, steps, depth, sizes),
        out_shape=jax.ShapeDtypeStruct(flat.shape, flat.dtype),
        in_specs=[pl.BlockSpec(memory_space=pltpu.HBM)] * 8,
        out_specs=pl.BlockSpec(memory_space=pl.ANY),
        scratch_shapes=[
            pltpu.VMEM((steps, CHUNK, rows, cols), flat.dtype),
            *[pltpu.VMEM((steps, CHUNK, rows, p[2] * BLK), flat.dtype) for p in pieces],
            pltpu.SMEM(band_counts.shape, jnp.int32),
            pltpu.SMEM(dep_blocks.shape, jnp.int32),
            *[
                pltpu.VMEM((rows, cols), kind.dtype)
                for kind in (lon_entry, lon_offset, lon_frac, lat_offset, lat_frac)
            ],
            pltpu.VMEM((n_src, CHUNK * rows, BLK), jnp.float32),
            pltpu.VMEM((11, rows, cols), jnp.float32),
            pltpu.VMEM((rows, n_src * BLK, cols), jnp.bfloat16),
            pltpu.VMEM((steps, rows + 4, CHUNK, cols), flat.dtype),
            pltpu.VMEM((blocks, CHUNK * rows, BLK), jnp.float32),
            pltpu.VMEM((steps, CHUNK, rows, cols), flat.dtype),
            dma((steps,)),
            dma((n_pieces, steps)),
            dma((n_pieces, steps)),
            dma((2, steps)),
            dma((2, steps)),
            dma((steps,)),
            dma((steps,)),
            dma((steps,)),
            dma(()),
            dma(()),
            dma((7,)),
        ],
        compiler_params=pltpu.CompilerParams(
            collective_id=0, has_side_effects=True, vmem_limit_bytes=67043328
        ),
    )(flat, band_counts, dep_blocks, lon_entry, lon_offset, lon_frac, lat_offset, lat_frac)
    moved = jnp.where(lax.axis_index("tm") > 0, prev.astype(jnp.float32), 0.0)
    misfit = (flat.astype(jnp.float32) - moved).astype(state.dtype)
    return misfit.reshape(state.shape)


def solution(mesh):
    placed = (
        P("tm", None, None, "lat", "lon"),
        P("tm", "lat"),
        P("tm", "lat", "lon", None),
        P("tm", "lat", "lon"),
        P("tm", "lat", "lon"),
        P("tm", "lat", "lon"),
        P("tm", "lat", "lon"),
        P("tm", "lat", "lon"),
    )
    sizes = tuple(mesh.shape[name] for name in ("tm", "lat", "lon"))
    return jax.shard_map(
        functools.partial(body, sizes),
        mesh=mesh,
        in_specs=placed,
        out_specs=P("tm", None, None, "lat", "lon"),
        check_vma=False,
    )
```

```python
import functools

import jax
import jax.numpy as jnp
from jax import lax
from jax.experimental import pallas as pl
from jax.experimental.pallas import tpu as pltpu
from jax.sharding import PartitionSpec as P

BLK = 128
CHUNK = 72
MESH = pl.DeviceIdType.MESH


def cubic_weights(fraction):
    return [
        -fraction * (fraction - 1.0) * (fraction - 2.0) / 6.0,
        (fraction + 1.0) * (fraction - 1.0) * (fraction - 2.0) / 2.0,
        -(fraction + 1.0) * fraction * (fraction - 2.0) / 2.0,
        (fraction + 1.0) * fraction * (fraction - 1.0) / 6.0,
    ]


def source_plan(blocks, devices):
    spread = blocks + blocks // 2
    count = min(3 * blocks, blocks * devices)
    slots, pieces, at = [None] * count, [], blocks
    for q in range(count):
        offset, block = divmod(q - spread, blocks)
        if offset % devices == 0:
            slots[q] = block
            continue
        if pieces and pieces[-1][0] == offset and pieces[-1][1] + pieces[-1][2] == block:
            pieces[-1][2] += 1
        else:
            pieces.append([offset, block, 1, at])
        slots[q] = at
        at += 1
    return slots, [tuple(piece) for piece in pieces], at


def kernel(plan, steps, depth, sizes, state, counts, lists, *rest_refs):
    slots, pieces, n_src = plan
    arrays, prev, scratch = rest_refs[:5], rest_refs[5], rest_refs[6:]
    n_tm, n_lat, n_lon = sizes
    n_pieces = len(pieces)
    own, remotes = scratch[0], scratch[1 : 1 + n_pieces]
    (
        counts_s, lists_s, *arrays_v, flat, params, matrix, adv, f_end, ends, own_sem, x_send, x_recv,
        h_send, h_recv, t_send, t_recv, raw_send, p_send, p_recv, a_sem,
    ) = scratch[1 + n_pieces :]
    rows, cols = state.shape[1:]
    tm, lat, lon = lax.axis_index("tm"), lax.axis_index("lat"), lax.axis_index("lon")

    helping = n_tm >= 3
    helper, helped = n_tm - 1, n_tm - 3
    half = steps // 2
    rest = depth - (steps - 1) * CHUNK
    is_helper = tm == helper
    if helping:
        first = jnp.where(is_helper, half, 0)
        last = jnp.where(tm == helped, half, steps)
        target = jnp.where(is_helper, helped + 1, tm + 1)
    else:
        first = 0
        last = jnp.where(is_helper, 0, steps)
        target = tm + 1

    barrier = pltpu.get_barrier_semaphore()
    lon_near = sorted({p[0] % n_lon for p in pieces} | {-p[0] % n_lon for p in pieces})
    greeted = len(lon_near)
    for o in lon_near:
        pl.semaphore_signal(
            barrier, inc=1, device_id={"lon": lax.rem(lon + o, n_lon)}, device_id_type=MESH
        )

    def greet(condition, device):
        @pl.when(condition)
        def _():
            pl.semaphore_signal(barrier, inc=1, device_id=device, device_id_type=MESH)

        return jnp.where(condition, 1, 0)

    greeted += greet(lat > 0, {"lat": lat - 1}) + greet(lat < n_lat - 1, {"lat": lat + 1})
    greeted += greet(tm > 0, {"tm": tm - 1}) + greet(tm < n_tm - 1, {"tm": tm + 1})
    if helping:
        greeted += greet(tm == helped, {"tm": helper}) + greet(is_helper, {"tm": helped})
    pl.semaphore_wait(barrier, greeted)

    def begin(c):
        return jnp.minimum(c * CHUNK, depth - CHUNK)

    def own_copy(c):
        return pltpu.make_async_copy(state.at[pl.ds(begin(c), CHUNK)], own.at[c], own_sem.at[c])

    def raw_copy(c):
        return pltpu.make_async_remote_copy(
            src_ref=state.at[pl.ds(begin(c), CHUNK)], dst_ref=own.at[c], send_sem=raw_send.at[c],
            recv_sem=own_sem.at[c], device_id={"tm": helper}, device_id_type=MESH,
        )

    def prm_copy():
        return pltpu.make_async_remote_copy(
            src_ref=params, dst_ref=params, send_sem=p_send, recv_sem=p_recv,
            device_id={"tm": helper}, device_id_type=MESH,
        )

    def x_copies(c, short, source=None):
        source = own.at[c] if source is None else source
        part = pl.ds(CHUNK - rest, rest) if short else pl.ds(0, CHUNK)
        copies = []
        for i, (offset, block, number, _) in enumerate(pieces):
            copies.append(
                pltpu.make_async_remote_copy(
                    src_ref=source.at[part, :, pl.ds(block * BLK, number * BLK)],
                    dst_ref=remotes[i].at[c, part],
                    send_sem=x_send.at[i, c], recv_sem=x_recv.at[i, c],
                    device_id={"lon": lax.rem(lon - offset + 2 * n_lon, n_lon)},
                    device_id_type=MESH,
                )
            )
        return copies

    def each_x(c, act, source=None):
        @pl.when(c < steps - 1)
        def _():
            for copy in x_copies(c, False, source):
                act(copy)

        @pl.when(c == steps - 1)
        def _():
            for copy in x_copies(c, True, source):
                act(copy)

    def halo_up(c):
        return pltpu.make_async_remote_copy(
            src_ref=adv.at[c, pl.ds(rows, 2)], dst_ref=adv.at[c, pl.ds(0, 2)],
            send_sem=h_send.at[0, c], recv_sem=h_recv.at[0, c],
            device_id={"lat": lat + 1}, device_id_type=MESH,
        )

    def halo_down(c):
        return pltpu.make_async_remote_copy(
            src_ref=adv.at[c, pl.ds(2, 2)], dst_ref=adv.at[c, pl.ds(rows + 2, 2)],
            send_sem=h_send.at[1, c], recv_sem=h_recv.at[1, c],
            device_id={"lat": lat - 1}, device_id_type=MESH,
        )

    def end_copy(c, short):
        if short:
            source, place = ends.at[c, pl.ds(CHUNK - rest, rest)], pl.ds((steps - 1) * CHUNK, rest)
        else:
            source, place = ends.at[c], pl.ds(c * CHUNK, CHUNK)
        return pltpu.make_async_remote_copy(
            src_ref=source, dst_ref=prev.at[place], send_sem=t_send.at[c], recv_sem=t_recv.at[c],
            device_id={"tm": target}, device_id_type=MESH,
        )

    def each_end(c, act):
        @pl.when(c < steps - 1)
        def _():
            act(end_copy(c, False))

        @pl.when(c == steps - 1)
        def _():
            act(end_copy(c, True))

    def loop(low, high, act):
        lax.fori_loop(low, high, lambda c, _: (act(c), 0)[1], 0)

    aux = [
        pltpu.make_async_copy(source, place, a_sem.at[i])
        for i, (source, place) in enumerate(
            [(counts, counts_s), (lists, lists_s)]
            + [(array.at[0], place) for array, place in zip(arrays, arrays_v)]
        )
    ]
    local = jnp.logical_not(is_helper)

    @pl.when(local)
    def _():
        def send(c):
            each_x(c, lambda copy: copy.start(), state.at[pl.ds(begin(c), CHUNK)])

        loop(first, jnp.minimum(first + 1, last), send)
        loop(first, last, lambda c: own_copy(c).start())
        loop(jnp.minimum(first + 1, last), last, send)
        for copy in aux:
            copy.start()

    if helping:

        @pl.when(tm == helped)
        def _():
            loop(half, steps, lambda c: raw_copy(c).start())

    def forward(c):
        own_copy(c).wait()
        each_x(c, lambda copy: copy.start())

    ahead = 2

    @pl.when(is_helper)
    def _():
        loop(first, jnp.minimum(first + ahead, last), forward)

    @pl.when(lat == 0)
    def _():
        adv[:, 0:2] = jnp.zeros((steps, 2, CHUNK, cols), adv.dtype)

    @pl.when(lat == n_lat - 1)
    def _():
        adv[:, rows + 2 : rows + 4] = jnp.zeros((steps, 2, CHUNK, cols), adv.dtype)

    def prepare():
        for copy in aux:
            copy.wait()
        entry, offset, lon_fraction, lat_shift, lat_fraction = [v[...] for v in arrays_v]
        per_list = lists.shape[1]
        for _ in range((per_list - 1) // 2):
            entry = jnp.where(entry >= counts_s[0, 0], entry - counts_s[0, 0], entry)
        blocks = cols // BLK
        total = blocks * n_lon
        for r in range(rows):
            for g in range(blocks):
                wanted = entry[r : r + 1, g * BLK : (g + 1) * BLK]
                chosen = jnp.zeros((1, BLK), jnp.int32)
                for k in range(per_list):
                    q = lists_s[0, k, g, r] - lon * blocks + blocks + blocks // 2 + total
                    q = lax.rem(q, total)
                    slot = jnp.int32(slots[0])
                    for i in range(1, len(slots)):
                        slot = jnp.where(q == i, slots[i], slot)
                    chosen = jnp.where(wanted == k, slot, chosen)
                params[1, r : r + 1, g * BLK : (g + 1) * BLK] = chosen.astype(jnp.float32)
        params[0] = offset.astype(jnp.float32)
        for node, weight in enumerate(cubic_weights(lon_fraction)):
            params[2 + node] = weight.astype(jnp.bfloat16).astype(jnp.float32)
        lat_weights = cubic_weights(lat_fraction)
        for shift in range(-2, 3):
            coefficient = jnp.zeros((rows, cols), jnp.float32)
            for node in range(4):
                coefficient = coefficient + jnp.where(
                    lat_shift + node - 1 == shift, lat_weights[node], 0.0
                )
            params[8 + shift] = coefficient

    def build(r):
        offset, slot = params[0, pl.ds(r, 1), :], params[1, pl.ds(r, 1), :]
        gap = lax.broadcasted_iota(jnp.int32, (BLK, cols), 0).astype(jnp.float32) - offset
        value = jnp.zeros((BLK, cols), jnp.float32)
        for node in range(4):
            weight = params[2 + node, pl.ds(r, 1), :]
            value = jnp.where(gap == node - 1.0, weight, value)
        for q in range(n_src):
            matrix[r, q * BLK : (q + 1) * BLK, :] = jnp.where(slot == q, value, 0.0).astype(
                jnp.bfloat16
            )

    def advect(c):
        @pl.when(local)
        def _():
            own_copy(c).wait()

        each_x(c, lambda copy: copy.wait_recv())
        at = 0
        for buffer in (own, *remotes):
            for b in range(buffer.shape[3] // BLK):
                part = buffer[c, :, :, b * BLK : (b + 1) * BLK].astype(jnp.float32)
                flat[at] = part.reshape(CHUNK * rows, BLK)
                at += 1
        for r in [0, 1, rows - 2, rows - 1] + list(range(2, rows - 2)):
            parts = [
                flat[q, pl.ds(r, CHUNK, stride=rows), :].astype(jnp.bfloat16)
                for q in range(n_src)
            ]
            total = jnp.dot(
                jnp.concatenate(parts, axis=1), matrix[r], preferred_element_type=jnp.float32
            )
            adv[c, r + 2] = total.astype(adv.dtype)
            if r == 2:

                @pl.when(lat < n_lat - 1)
                def _():
                    halo_up(c).start()

                @pl.when(lat > 0)
                def _():
                    halo_down(c).start()

    def finish(c):
        def interpolate(r):
            total = None
            for shift in range(5):
                term = params[6 + shift, r : r + 1, :] * adv[c, r + shift].astype(jnp.float32)
                total = term if total is None else total + term
            for b in range(cols // BLK):
                f_end[b, pl.ds(r, CHUNK, stride=rows), :] = total[:, b * BLK : (b + 1) * BLK]

        for r in range(2, rows - 2):
            interpolate(r)

        @pl.when(lat > 0)
        def _():
            halo_up(c).wait_recv()

        @pl.when(lat < n_lat - 1)
        def _():
            halo_down(c).wait_recv()

        for r in (0, 1, rows - 2, rows - 1):
            interpolate(r)
        for b in range(cols // BLK):
            part = f_end[b].reshape(CHUNK, rows, BLK).astype(ends.dtype)
            ends[c, :, :, b * BLK : (b + 1) * BLK] = part
        each_end(c, lambda copy: copy.start())

    def step(c):
        @pl.when(jnp.logical_and(is_helper, c + ahead < last))
        def _():
            forward(c + ahead)

        @pl.when(c < last)
        def _():
            advect(c)

        @pl.when(c > first)
        def _():
            finish(c - 1)

    def settle(c):
        each_x(c, lambda copy: copy.wait_send())

        @pl.when(lat < n_lat - 1)
        def _():
            halo_up(c).wait_send()

        @pl.when(lat > 0)
        def _():
            halo_down(c).wait_send()

        each_end(c, lambda copy: copy.wait_send())

    @pl.when(first < last)
    def _():
        pl.when(local)(prepare)
        if helping:

            @pl.when(tm == helped)
            def _():
                prm_copy().start()

            @pl.when(is_helper)
            def _():
                prm_copy().wait_recv()

        loop(0, rows, build)
        loop(first, last + 1, step)
        loop(first, last, settle)

    if helping:

        @pl.when(tm == helped)
        def _():
            prm_copy().wait_send()
            loop(half, steps, lambda c: raw_copy(c).wait_send())

    @pl.when(tm > 0)
    def _():
        loop(0, steps, lambda c: each_end(c, lambda copy: copy.wait_recv()))


def body(sizes, state, band_counts, dep_blocks, lon_entry, lon_offset, lon_frac, lat_offset, lat_frac):
    fields_n, levels, rows, cols = state.shape[1:]
    depth, blocks = fields_n * levels, cols // BLK
    n_tm, n_lat, n_lon = sizes
    plan = source_plan(blocks, n_lon)
    _, pieces, n_src = plan
    steps = -(-depth // CHUNK)
    flat = state.reshape(depth, rows, cols)

    lists = jnp.transpose(dep_blocks, (0, 3, 2, 1))
    dma = pltpu.SemaphoreType.DMA
    n_pieces = len(pieces)
    prev = pl.pallas_call(
        functools.partial(kernel, plan, steps, depth, sizes),
        out_shape=pltpu.VMEM(flat.shape, flat.dtype),
        in_specs=[pl.BlockSpec(memory_space=pltpu.HBM)] * 8,
        out_specs=pl.BlockSpec(memory_space=pl.ANY),
        scratch_shapes=[
            pltpu.VMEM((steps, CHUNK, rows, cols), flat.dtype),
            *[pltpu.VMEM((steps, CHUNK, rows, p[2] * BLK), flat.dtype) for p in pieces],
            pltpu.SMEM(band_counts.shape, jnp.int32),
            pltpu.SMEM(lists.shape, jnp.int32),
            *[
                pltpu.VMEM((rows, cols), kind.dtype)
                for kind in (lon_entry, lon_offset, lon_frac, lat_offset, lat_frac)
            ],
            pltpu.VMEM((n_src, CHUNK * rows, BLK), jnp.float32),
            pltpu.VMEM((11, rows, cols), jnp.float32),
            pltpu.VMEM((rows, n_src * BLK, cols), jnp.bfloat16),
            pltpu.VMEM((steps, rows + 4, CHUNK, cols), flat.dtype),
            pltpu.VMEM((blocks, CHUNK * rows, BLK), jnp.float32),
            pltpu.VMEM((steps, CHUNK, rows, cols), flat.dtype),
            dma((steps,)),
            dma((n_pieces, steps)),
            dma((n_pieces, steps)),
            dma((2, steps)),
            dma((2, steps)),
            dma((steps,)),
            dma((steps,)),
            dma((steps,)),
            dma(()),
            dma(()),
            dma((7,)),
        ],
        compiler_params=pltpu.CompilerParams(
            collective_id=0, has_side_effects=True, vmem_limit_bytes=60 * 1024 * 1024
        ),
    )(
        pltpu.with_memory_space_constraint(flat, pltpu.HBM),
        band_counts,
        *[
            pltpu.with_memory_space_constraint(array, pltpu.HBM)
            for array in (lists, lon_entry, lon_offset, lon_frac, lat_offset, lat_frac)
        ],
    )
    moved = jnp.where(lax.axis_index("tm") > 0, prev.astype(jnp.float32), 0.0)
    misfit = (flat.astype(jnp.float32) - moved).astype(state.dtype)
    return misfit.reshape(state.shape)


def solution(mesh):
    placed = (
        P("tm", None, None, "lat", "lon"),
        P("tm", "lat"),
        P("tm", "lat", "lon", None),
        P("tm", "lat", "lon"),
        P("tm", "lat", "lon"),
        P("tm", "lat", "lon"),
        P("tm", "lat", "lon"),
        P("tm", "lat", "lon"),
    )
    sizes = tuple(mesh.shape[name] for name in ("tm", "lat", "lon"))
    return jax.shard_map(
        functools.partial(body, sizes),
        mesh=mesh,
        in_specs=placed,
        out_specs=P("tm", None, None, "lat", "lon"),
        check_vma=False,
    )
```

```python
import functools

import jax
import jax.numpy as jnp
from jax import lax
from jax.experimental import pallas as pl
from jax.experimental.pallas import tpu as pltpu
from jax.sharding import PartitionSpec as P

BLK = 128
CHUNK = 72
MESH = pl.DeviceIdType.MESH


def cubic_weights(fraction):
    return [
        -fraction * (fraction - 1.0) * (fraction - 2.0) / 6.0,
        (fraction + 1.0) * (fraction - 1.0) * (fraction - 2.0) / 2.0,
        -(fraction + 1.0) * fraction * (fraction - 2.0) / 2.0,
        (fraction + 1.0) * fraction * (fraction - 1.0) / 6.0,
    ]


def source_plan(blocks, devices):
    spread = blocks + blocks // 2
    count = min(3 * blocks, blocks * devices)
    slots, pieces, at = [None] * count, [], blocks
    for q in range(count):
        offset, block = divmod(q - spread, blocks)
        if offset % devices == 0:
            slots[q] = block
            continue
        if pieces and pieces[-1][0] == offset and pieces[-1][1] + pieces[-1][2] == block:
            pieces[-1][2] += 1
        else:
            pieces.append([offset, block, 1, at])
        slots[q] = at
        at += 1
    return slots, [tuple(piece) for piece in pieces], at


def kernel(plan, steps, depth, sizes, state, counts, lists, *rest_refs):
    slots, pieces, n_src = plan
    arrays, result, scratch = rest_refs[:5], rest_refs[5], rest_refs[6:]
    n_tm, n_lat, n_lon = sizes
    n_pieces = len(pieces)
    own, remotes = scratch[0], scratch[1 : 1 + n_pieces]
    (
        mine, prev, m_sem, counts_s, lists_s, *arrays_v, flat, params, matrix, adv, f_end, ends, own_sem, x_send, x_recv,
        h_send, h_recv, t_send, t_recv, raw_send, p_send, p_recv, a_sem,
    ) = scratch[1 + n_pieces :]
    rows, cols = state.shape[1:]
    tm, lat, lon = lax.axis_index("tm"), lax.axis_index("lat"), lax.axis_index("lon")

    helping = n_tm >= 3
    helper, helped = n_tm - 1, n_tm - 3
    half = steps // 2
    rest = depth - (steps - 1) * CHUNK
    is_helper = tm == helper
    if helping:
        first = jnp.where(is_helper, half, 0)
        last = jnp.where(tm == helped, half, steps)
        target = jnp.where(is_helper, helped + 1, tm + 1)
    else:
        first = 0
        last = jnp.where(is_helper, 0, steps)
        target = tm + 1

    barrier = pltpu.get_barrier_semaphore()
    lon_near = sorted({p[0] % n_lon for p in pieces} | {-p[0] % n_lon for p in pieces})
    greeted = len(lon_near)
    for o in lon_near:
        pl.semaphore_signal(
            barrier, inc=1, device_id={"lon": lax.rem(lon + o, n_lon)}, device_id_type=MESH
        )

    def greet(condition, device):
        @pl.when(condition)
        def _():
            pl.semaphore_signal(barrier, inc=1, device_id=device, device_id_type=MESH)

        return jnp.where(condition, 1, 0)

    greeted += greet(lat > 0, {"lat": lat - 1}) + greet(lat < n_lat - 1, {"lat": lat + 1})
    greeted += greet(tm > 0, {"tm": tm - 1}) + greet(tm < n_tm - 1, {"tm": tm + 1})
    if helping:
        greeted += greet(tm == helped, {"tm": helper}) + greet(is_helper, {"tm": helped})
    pl.semaphore_wait(barrier, greeted)

    def begin(c):
        return jnp.minimum(c * CHUNK, depth - CHUNK)

    def own_copy(c):
        return pltpu.make_async_copy(state.at[pl.ds(begin(c), CHUNK)], own.at[c], own_sem.at[c])

    def raw_copy(c):
        return pltpu.make_async_remote_copy(
            src_ref=state.at[pl.ds(begin(c), CHUNK)], dst_ref=own.at[c], send_sem=raw_send.at[c],
            recv_sem=own_sem.at[c], device_id={"tm": helper}, device_id_type=MESH,
        )

    def prm_copy():
        return pltpu.make_async_remote_copy(
            src_ref=params, dst_ref=params, send_sem=p_send, recv_sem=p_recv,
            device_id={"tm": helper}, device_id_type=MESH,
        )

    def x_copies(c, short, source=None):
        source = own.at[c] if source is None else source
        part = pl.ds(CHUNK - rest, rest) if short else pl.ds(0, CHUNK)
        copies = []
        for i, (offset, block, number, _) in enumerate(pieces):
            copies.append(
                pltpu.make_async_remote_copy(
                    src_ref=source.at[part, :, pl.ds(block * BLK, number * BLK)],
                    dst_ref=remotes[i].at[c, part],
                    send_sem=x_send.at[i, c], recv_sem=x_recv.at[i, c],
                    device_id={"lon": lax.rem(lon - offset + 2 * n_lon, n_lon)},
                    device_id_type=MESH,
                )
            )
        return copies

    def each_x(c, act, source=None):
        @pl.when(c < steps - 1)
        def _():
            for copy in x_copies(c, False, source):
                act(copy)

        @pl.when(c == steps - 1)
        def _():
            for copy in x_copies(c, True, source):
                act(copy)

    def halo_up(c):
        return pltpu.make_async_remote_copy(
            src_ref=adv.at[c, pl.ds(rows, 2)], dst_ref=adv.at[c, pl.ds(0, 2)],
            send_sem=h_send.at[0, c], recv_sem=h_recv.at[0, c],
            device_id={"lat": lat + 1}, device_id_type=MESH,
        )

    def halo_down(c):
        return pltpu.make_async_remote_copy(
            src_ref=adv.at[c, pl.ds(2, 2)], dst_ref=adv.at[c, pl.ds(rows + 2, 2)],
            send_sem=h_send.at[1, c], recv_sem=h_recv.at[1, c],
            device_id={"lat": lat - 1}, device_id_type=MESH,
        )

    def end_copy(c, short):
        if short:
            source, place = ends.at[c, pl.ds(CHUNK - rest, rest)], pl.ds((steps - 1) * CHUNK, rest)
        else:
            source, place = ends.at[c], pl.ds(c * CHUNK, CHUNK)
        return pltpu.make_async_remote_copy(
            src_ref=source, dst_ref=prev.at[place], send_sem=t_send.at[c], recv_sem=t_recv.at[c],
            device_id={"tm": target}, device_id_type=MESH,
        )

    def each_end(c, act):
        @pl.when(c < steps - 1)
        def _():
            act(end_copy(c, False))

        @pl.when(c == steps - 1)
        def _():
            act(end_copy(c, True))

    def loop(low, high, act):
        lax.fori_loop(low, high, lambda c, _: (act(c), 0)[1], 0)

    aux = [
        pltpu.make_async_copy(source, place, a_sem.at[i])
        for i, (source, place) in enumerate(
            [(counts, counts_s), (lists, lists_s)]
            + [(array.at[0], place) for array, place in zip(arrays, arrays_v)]
        )
    ]
    local = jnp.logical_not(is_helper)

    @pl.when(local)
    def _():
        def send(c):
            each_x(c, lambda copy: copy.start(), state.at[pl.ds(begin(c), CHUNK)])

        loop(first, jnp.minimum(first + 1, last), send)
        loop(first, last, lambda c: own_copy(c).start())
        loop(jnp.minimum(first + 1, last), last, send)
        for copy in aux:
            copy.start()

    if helping:

        @pl.when(tm == helped)
        def _():
            loop(half, steps, lambda c: raw_copy(c).start())

    def forward(c):
        own_copy(c).wait()
        each_x(c, lambda copy: copy.start())

    to_mine = pltpu.make_async_copy(state, mine, m_sem)
    to_result = pltpu.make_async_copy(state, result, m_sem)
    pl.when(tm > 0)(to_mine.start)
    pl.when(tm == 0)(to_result.start)

    ahead = 2

    @pl.when(is_helper)
    def _():
        loop(first, jnp.minimum(first + ahead, last), forward)

    @pl.when(lat == 0)
    def _():
        adv[:, 0:2] = jnp.zeros((steps, 2, CHUNK, cols), adv.dtype)

    @pl.when(lat == n_lat - 1)
    def _():
        adv[:, rows + 2 : rows + 4] = jnp.zeros((steps, 2, CHUNK, cols), adv.dtype)

    def prepare():
        for copy in aux:
            copy.wait()
        entry, offset, lon_fraction, lat_shift, lat_fraction = [v[...] for v in arrays_v]
        per_list = lists.shape[1]
        for _ in range((per_list - 1) // 2):
            entry = jnp.where(entry >= counts_s[0, 0], entry - counts_s[0, 0], entry)
        blocks = cols // BLK
        total = blocks * n_lon
        for r in range(rows):
            for g in range(blocks):
                wanted = entry[r : r + 1, g * BLK : (g + 1) * BLK]
                chosen = jnp.zeros((1, BLK), jnp.int32)
                for k in range(per_list):
                    q = lists_s[0, k, g, r] - lon * blocks + blocks + blocks // 2 + total
                    q = lax.rem(q, total)
                    slot = jnp.int32(slots[0])
                    for i in range(1, len(slots)):
                        slot = jnp.where(q == i, slots[i], slot)
                    chosen = jnp.where(wanted == k, slot, chosen)
                params[1, r : r + 1, g * BLK : (g + 1) * BLK] = chosen.astype(jnp.float32)
        params[0] = offset.astype(jnp.float32)
        for node, weight in enumerate(cubic_weights(lon_fraction)):
            params[2 + node] = weight.astype(jnp.bfloat16).astype(jnp.float32)
        lat_weights = cubic_weights(lat_fraction)
        for shift in range(-2, 3):
            coefficient = jnp.zeros((rows, cols), jnp.float32)
            for node in range(4):
                coefficient = coefficient + jnp.where(
                    lat_shift + node - 1 == shift, lat_weights[node], 0.0
                )
            params[8 + shift] = coefficient

    def build(r):
        offset, slot = params[0, pl.ds(r, 1), :], params[1, pl.ds(r, 1), :]
        gap = lax.broadcasted_iota(jnp.int32, (BLK, cols), 0).astype(jnp.float32) - offset
        value = jnp.zeros((BLK, cols), jnp.float32)
        for node in range(4):
            weight = params[2 + node, pl.ds(r, 1), :]
            value = jnp.where(gap == node - 1.0, weight, value)
        for q in range(n_src):
            matrix[r, q * BLK : (q + 1) * BLK, :] = jnp.where(slot == q, value, 0.0).astype(
                jnp.bfloat16
            )

    def advect(c):
        @pl.when(local)
        def _():
            own_copy(c).wait()

        each_x(c, lambda copy: copy.wait_recv())
        at = 0
        for buffer in (own, *remotes):
            for b in range(buffer.shape[3] // BLK):
                part = buffer[c, :, :, b * BLK : (b + 1) * BLK].astype(jnp.float32)
                flat[at] = part.reshape(CHUNK * rows, BLK)
                at += 1
        for r in [0, 1, rows - 2, rows - 1] + list(range(2, rows - 2)):
            parts = [
                flat[q, pl.ds(r, CHUNK, stride=rows), :].astype(jnp.bfloat16)
                for q in range(n_src)
            ]
            total = jnp.dot(
                jnp.concatenate(parts, axis=1), matrix[r], preferred_element_type=jnp.float32
            )
            adv[c, r + 2] = total.astype(adv.dtype)
            if r == 2:

                @pl.when(lat < n_lat - 1)
                def _():
                    halo_up(c).start()

                @pl.when(lat > 0)
                def _():
                    halo_down(c).start()

    def finish(c):
        def interpolate(r):
            total = None
            for shift in range(5):
                term = params[6 + shift, r : r + 1, :] * adv[c, r + shift].astype(jnp.float32)
                total = term if total is None else total + term
            for b in range(cols // BLK):
                f_end[b, pl.ds(r, CHUNK, stride=rows), :] = total[:, b * BLK : (b + 1) * BLK]

        for r in range(2, rows - 2):
            interpolate(r)

        @pl.when(lat > 0)
        def _():
            halo_up(c).wait_recv()

        @pl.when(lat < n_lat - 1)
        def _():
            halo_down(c).wait_recv()

        for r in (0, 1, rows - 2, rows - 1):
            interpolate(r)
        for b in range(cols // BLK):
            part = f_end[b].reshape(CHUNK, rows, BLK).astype(ends.dtype)
            ends[c, :, :, b * BLK : (b + 1) * BLK] = part
        each_end(c, lambda copy: copy.start())

    def step(c):
        @pl.when(jnp.logical_and(is_helper, c + ahead < last))
        def _():
            forward(c + ahead)

        @pl.when(c < last)
        def _():
            advect(c)

        @pl.when(c > first)
        def _():
            finish(c - 1)

    def settle(c):
        each_x(c, lambda copy: copy.wait_send())

        @pl.when(lat < n_lat - 1)
        def _():
            halo_up(c).wait_send()

        @pl.when(lat > 0)
        def _():
            halo_down(c).wait_send()

        each_end(c, lambda copy: copy.wait_send())

    @pl.when(first < last)
    def _():
        pl.when(local)(prepare)
        if helping:

            @pl.when(tm == helped)
            def _():
                prm_copy().start()

            @pl.when(is_helper)
            def _():
                prm_copy().wait_recv()

        loop(0, rows, build)
        loop(first, last + 1, step)

    def subtract(place):
        moved = prev[place].astype(jnp.float32)
        result[place] = (mine[place].astype(jnp.float32) - moved).astype(result.dtype)

    @pl.when(tm > 0)
    def _():
        to_mine.wait()

        def collect(c):
            end_copy(c, False).wait_recv()
            subtract(pl.ds(c * CHUNK, CHUNK))

        loop(0, steps - 1, collect)
        end_copy(steps - 1, True).wait_recv()
        subtract(pl.ds((steps - 1) * CHUNK, rest))

    pl.when(tm == 0)(to_result.wait)
    loop(first, last, settle)
    if helping:

        @pl.when(tm == helped)
        def _():
            prm_copy().wait_send()
            loop(half, steps, lambda c: raw_copy(c).wait_send())


def body(sizes, state, band_counts, dep_blocks, lon_entry, lon_offset, lon_frac, lat_offset, lat_frac):
    fields_n, levels, rows, cols = state.shape[1:]
    depth, blocks = fields_n * levels, cols // BLK
    n_tm, n_lat, n_lon = sizes
    plan = source_plan(blocks, n_lon)
    _, pieces, n_src = plan
    steps = -(-depth // CHUNK)
    flat = state.reshape(depth, rows, cols)

    lists = jnp.transpose(dep_blocks, (0, 3, 2, 1))
    dma = pltpu.SemaphoreType.DMA
    n_pieces = len(pieces)
    misfit = pl.pallas_call(
        functools.partial(kernel, plan, steps, depth, sizes),
        out_shape=pltpu.VMEM(flat.shape, flat.dtype),
        in_specs=[pl.BlockSpec(memory_space=pltpu.HBM)] * 8,
        out_specs=pl.BlockSpec(memory_space=pltpu.VMEM),
        scratch_shapes=[
            pltpu.VMEM((steps, CHUNK, rows, cols), flat.dtype),
            *[pltpu.VMEM((steps, CHUNK, rows, p[2] * BLK), flat.dtype) for p in pieces],
            pltpu.VMEM(flat.shape, flat.dtype),
            pltpu.VMEM(flat.shape, flat.dtype),
            dma(()),
            pltpu.SMEM(band_counts.shape, jnp.int32),
            pltpu.SMEM(lists.shape, jnp.int32),
            *[
                pltpu.VMEM((rows, cols), kind.dtype)
                for kind in (lon_entry, lon_offset, lon_frac, lat_offset, lat_frac)
            ],
            pltpu.VMEM((n_src, CHUNK * rows, BLK), jnp.float32),
            pltpu.VMEM((11, rows, cols), jnp.float32),
            pltpu.VMEM((rows, n_src * BLK, cols), jnp.bfloat16),
            pltpu.VMEM((steps, rows + 4, CHUNK, cols), flat.dtype),
            pltpu.VMEM((blocks, CHUNK * rows, BLK), jnp.float32),
            pltpu.VMEM((steps, CHUNK, rows, cols), flat.dtype),
            dma((steps,)),
            dma((n_pieces, steps)),
            dma((n_pieces, steps)),
            dma((2, steps)),
            dma((2, steps)),
            dma((steps,)),
            dma((steps,)),
            dma((steps,)),
            dma(()),
            dma(()),
            dma((7,)),
        ],
        compiler_params=pltpu.CompilerParams(
            collective_id=0, has_side_effects=True, vmem_limit_bytes=60 * 1024 * 1024
        ),
    )(
        pltpu.with_memory_space_constraint(flat, pltpu.HBM),
        band_counts,
        *[
            pltpu.with_memory_space_constraint(array, pltpu.HBM)
            for array in (lists, lon_entry, lon_offset, lon_frac, lat_offset, lat_frac)
        ],
    )
    return misfit.reshape(state.shape)


def solution(mesh):
    placed = (
        P("tm", None, None, "lat", "lon"),
        P("tm", "lat"),
        P("tm", "lat", "lon", None),
        P("tm", "lat", "lon"),
        P("tm", "lat", "lon"),
        P("tm", "lat", "lon"),
        P("tm", "lat", "lon"),
        P("tm", "lat", "lon"),
    )
    sizes = tuple(mesh.shape[name] for name in ("tm", "lat", "lon"))
    return jax.shard_map(
        functools.partial(body, sizes),
        mesh=mesh,
        in_specs=placed,
        out_specs=P("tm", None, None, "lat", "lon"),
        check_vma=False,
    )
```

```python
import functools

import jax
import jax.numpy as jnp
from jax import lax
from jax.experimental import pallas as pl
from jax.experimental.pallas import tpu as pltpu
from jax.sharding import PartitionSpec as P

BLK = 128
CHUNK = 56
MESH = pl.DeviceIdType.MESH


def cubic_weights(fraction):
    return [
        -fraction * (fraction - 1.0) * (fraction - 2.0) / 6.0,
        (fraction + 1.0) * (fraction - 1.0) * (fraction - 2.0) / 2.0,
        -(fraction + 1.0) * fraction * (fraction - 2.0) / 2.0,
        (fraction + 1.0) * fraction * (fraction - 1.0) / 6.0,
    ]


def source_plan(blocks, devices):
    spread = blocks + blocks // 2
    count = min(3 * blocks, blocks * devices)
    slots, pieces, at = [None] * count, [], blocks
    for q in range(count):
        offset, block = divmod(q - spread, blocks)
        if offset % devices == 0:
            slots[q] = block
            continue
        if pieces and pieces[-1][0] == offset and pieces[-1][1] + pieces[-1][2] == block:
            pieces[-1][2] += 1
        else:
            pieces.append([offset, block, 1, at])
        slots[q] = at
        at += 1
    return slots, [tuple(piece) for piece in pieces], at


def kernel(plan, steps, depth, sizes, state, counts, lists, *rest_refs):
    slots, pieces, n_src = plan
    arrays, result, scratch = rest_refs[:5], rest_refs[5], rest_refs[6:]
    n_tm, n_lat, n_lon = sizes
    n_pieces = len(pieces)
    own, remotes = scratch[0], scratch[1 : 1 + n_pieces]
    (
        mine, prev, m_sem, counts_s, lists_s, *arrays_v, flat, params, matrix, adv, f_end, ends, own_sem, x_send, x_recv,
        h_send, h_recv, t_send, t_recv, raw_send, p_send, p_recv, a_sem,
    ) = scratch[1 + n_pieces :]
    rows, cols = state.shape[1:]
    tm, lat, lon = lax.axis_index("tm"), lax.axis_index("lat"), lax.axis_index("lon")

    helping = n_tm >= 3
    helper, helped = n_tm - 1, n_tm - 3
    half = steps // 2
    rest = depth - (steps - 1) * CHUNK
    is_helper = tm == helper
    if helping:
        first = jnp.where(is_helper, half, 0)
        last = jnp.where(tm == helped, half, steps)
        target = jnp.where(is_helper, helped + 1, tm + 1)
    else:
        first = 0
        last = jnp.where(is_helper, 0, steps)
        target = tm + 1

    barrier = pltpu.get_barrier_semaphore()
    lon_near = sorted({p[0] % n_lon for p in pieces} | {-p[0] % n_lon for p in pieces})
    greeted = len(lon_near)
    for o in lon_near:
        pl.semaphore_signal(
            barrier, inc=1, device_id={"lon": lax.rem(lon + o, n_lon)}, device_id_type=MESH
        )

    def greet(condition, device):
        @pl.when(condition)
        def _():
            pl.semaphore_signal(barrier, inc=1, device_id=device, device_id_type=MESH)

        return jnp.where(condition, 1, 0)

    greeted += greet(lat > 0, {"lat": lat - 1}) + greet(lat < n_lat - 1, {"lat": lat + 1})
    greeted += greet(tm > 0, {"tm": tm - 1}) + greet(tm < n_tm - 1, {"tm": tm + 1})
    if helping:
        greeted += greet(tm == helped, {"tm": helper}) + greet(is_helper, {"tm": helped})
    pl.semaphore_wait(barrier, greeted)

    def begin(c):
        return jnp.minimum(c * CHUNK, depth - CHUNK)

    def own_copy(c):
        return pltpu.make_async_copy(state.at[pl.ds(begin(c), CHUNK)], own.at[c], own_sem.at[c])

    def raw_copy(c):
        return pltpu.make_async_remote_copy(
            src_ref=state.at[pl.ds(begin(c), CHUNK)], dst_ref=own.at[c], send_sem=raw_send.at[c],
            recv_sem=own_sem.at[c], device_id={"tm": helper}, device_id_type=MESH,
        )

    def prm_copy():
        return pltpu.make_async_remote_copy(
            src_ref=params, dst_ref=params, send_sem=p_send, recv_sem=p_recv,
            device_id={"tm": helper}, device_id_type=MESH,
        )

    def x_copies(c, short, source=None):
        source = own.at[c] if source is None else source
        part = pl.ds(CHUNK - rest, rest) if short else pl.ds(0, CHUNK)
        copies = []
        for i, (offset, block, number, _) in enumerate(pieces):
            copies.append(
                pltpu.make_async_remote_copy(
                    src_ref=source.at[part, :, pl.ds(block * BLK, number * BLK)],
                    dst_ref=remotes[i].at[c, part],
                    send_sem=x_send.at[i, c], recv_sem=x_recv.at[i, c],
                    device_id={"lon": lax.rem(lon - offset + 2 * n_lon, n_lon)},
                    device_id_type=MESH,
                )
            )
        return copies

    def each_x(c, act, source=None):
        @pl.when(c < steps - 1)
        def _():
            for copy in x_copies(c, False, source):
                act(copy)

        @pl.when(c == steps - 1)
        def _():
            for copy in x_copies(c, True, source):
                act(copy)

    def halo_up(c):
        return pltpu.make_async_remote_copy(
            src_ref=adv.at[c, pl.ds(rows, 2)], dst_ref=adv.at[c, pl.ds(0, 2)],
            send_sem=h_send.at[0, c], recv_sem=h_recv.at[0, c],
            device_id={"lat": lat + 1}, device_id_type=MESH,
        )

    def halo_down(c):
        return pltpu.make_async_remote_copy(
            src_ref=adv.at[c, pl.ds(2, 2)], dst_ref=adv.at[c, pl.ds(rows + 2, 2)],
            send_sem=h_send.at[1, c], recv_sem=h_recv.at[1, c],
            device_id={"lat": lat - 1}, device_id_type=MESH,
        )

    def end_copy(c, short):
        if short:
            source, place = ends.at[c, pl.ds(CHUNK - rest, rest)], pl.ds((steps - 1) * CHUNK, rest)
        else:
            source, place = ends.at[c], pl.ds(c * CHUNK, CHUNK)
        return pltpu.make_async_remote_copy(
            src_ref=source, dst_ref=prev.at[place], send_sem=t_send.at[c], recv_sem=t_recv.at[c],
            device_id={"tm": target}, device_id_type=MESH,
        )

    def each_end(c, act):
        @pl.when(c < steps - 1)
        def _():
            act(end_copy(c, False))

        @pl.when(c == steps - 1)
        def _():
            act(end_copy(c, True))

    def loop(low, high, act):
        lax.fori_loop(low, high, lambda c, _: (act(c), 0)[1], 0)

    aux = [
        pltpu.make_async_copy(source, place, a_sem.at[i])
        for i, (source, place) in enumerate(
            [(counts, counts_s), (lists, lists_s)]
            + [(array.at[0], place) for array, place in zip(arrays, arrays_v)]
        )
    ]
    local = jnp.logical_not(is_helper)

    @pl.when(local)
    def _():
        def send(c):
            each_x(c, lambda copy: copy.start(), state.at[pl.ds(begin(c), CHUNK)])

        loop(first, jnp.minimum(first + 1, last), send)
        loop(first, last, lambda c: own_copy(c).start())
        loop(jnp.minimum(first + 1, last), last, send)
        for copy in aux:
            copy.start()

    if helping:

        @pl.when(tm == helped)
        def _():
            loop(half, steps, lambda c: raw_copy(c).start())

    def forward(c):
        own_copy(c).wait()
        each_x(c, lambda copy: copy.start())

    to_mine = pltpu.make_async_copy(state, mine, m_sem)
    to_result = pltpu.make_async_copy(state, result, m_sem)
    pl.when(tm > 0)(to_mine.start)
    pl.when(tm == 0)(to_result.start)

    ahead = 2

    @pl.when(is_helper)
    def _():
        loop(first, jnp.minimum(first + ahead, last), forward)

    @pl.when(lat == 0)
    def _():
        adv[:, 0:2] = jnp.zeros((steps, 2, CHUNK, cols), adv.dtype)

    @pl.when(lat == n_lat - 1)
    def _():
        adv[:, rows + 2 : rows + 4] = jnp.zeros((steps, 2, CHUNK, cols), adv.dtype)

    def prepare():
        for copy in aux:
            copy.wait()
        entry, offset, lon_fraction, lat_shift, lat_fraction = [v[...] for v in arrays_v]
        per_list = lists.shape[1]
        for _ in range((per_list - 1) // 2):
            entry = jnp.where(entry >= counts_s[0, 0], entry - counts_s[0, 0], entry)
        blocks = cols // BLK
        total = blocks * n_lon
        for r in range(rows):
            for g in range(blocks):
                wanted = entry[r : r + 1, g * BLK : (g + 1) * BLK]
                chosen = jnp.zeros((1, BLK), jnp.int32)
                for k in range(per_list):
                    q = lists_s[0, k, g, r] - lon * blocks + blocks + blocks // 2 + total
                    q = lax.rem(q, total)
                    slot = jnp.int32(slots[0])
                    for i in range(1, len(slots)):
                        slot = jnp.where(q == i, slots[i], slot)
                    chosen = jnp.where(wanted == k, slot, chosen)
                params[1, r : r + 1, g * BLK : (g + 1) * BLK] = chosen.astype(jnp.float32)
        params[0] = offset.astype(jnp.float32)
        for node, weight in enumerate(cubic_weights(lon_fraction)):
            params[2 + node] = weight.astype(jnp.bfloat16).astype(jnp.float32)
        lat_weights = cubic_weights(lat_fraction)
        for shift in range(-2, 3):
            coefficient = jnp.zeros((rows, cols), jnp.float32)
            for node in range(4):
                coefficient = coefficient + jnp.where(
                    lat_shift + node - 1 == shift, lat_weights[node], 0.0
                )
            params[8 + shift] = coefficient

    def build(r):
        offset, slot = params[0, pl.ds(r, 1), :], params[1, pl.ds(r, 1), :]
        gap = lax.broadcasted_iota(jnp.int32, (BLK, cols), 0).astype(jnp.float32) - offset
        value = jnp.zeros((BLK, cols), jnp.float32)
        for node in range(4):
            weight = params[2 + node, pl.ds(r, 1), :]
            value = jnp.where(gap == node - 1.0, weight, value)
        for q in range(n_src):
            matrix[r, q * BLK : (q + 1) * BLK, :] = jnp.where(slot == q, value, 0.0).astype(
                jnp.bfloat16
            )

    def advect(c):
        @pl.when(local)
        def _():
            own_copy(c).wait()

        each_x(c, lambda copy: copy.wait_recv())
        at = 0
        for buffer in (own, *remotes):
            for b in range(buffer.shape[3] // BLK):
                part = buffer[c, :, :, b * BLK : (b + 1) * BLK].astype(jnp.float32)
                flat[at] = part.reshape(CHUNK * rows, BLK)
                at += 1
        for r in [0, 1, rows - 2, rows - 1] + list(range(2, rows - 2)):
            parts = [
                flat[q, pl.ds(r, CHUNK, stride=rows), :].astype(jnp.bfloat16)
                for q in range(n_src)
            ]
            total = jnp.dot(
                jnp.concatenate(parts, axis=1), matrix[r], preferred_element_type=jnp.float32
            )
            adv[c, r + 2] = total.astype(adv.dtype)
            if r == 2:

                @pl.when(lat < n_lat - 1)
                def _():
                    halo_up(c).start()

                @pl.when(lat > 0)
                def _():
                    halo_down(c).start()

    def finish(c):
        def interpolate(r):
            total = None
            for shift in range(5):
                term = params[6 + shift, r : r + 1, :] * adv[c, r + shift].astype(jnp.float32)
                total = term if total is None else total + term
            for b in range(cols // BLK):
                f_end[b, pl.ds(r, CHUNK, stride=rows), :] = total[:, b * BLK : (b + 1) * BLK]

        for r in range(2, rows - 2):
            interpolate(r)

        @pl.when(lat > 0)
        def _():
            halo_up(c).wait_recv()

        @pl.when(lat < n_lat - 1)
        def _():
            halo_down(c).wait_recv()

        for r in (0, 1, rows - 2, rows - 1):
            interpolate(r)
        for b in range(cols // BLK):
            part = f_end[b].reshape(CHUNK, rows, BLK).astype(ends.dtype)
            ends[c, :, :, b * BLK : (b + 1) * BLK] = part
        each_end(c, lambda copy: copy.start())

    def step(c):
        @pl.when(jnp.logical_and(is_helper, c + ahead < last))
        def _():
            forward(c + ahead)

        @pl.when(c < last)
        def _():
            advect(c)

        @pl.when(c > first)
        def _():
            finish(c - 1)

    def settle(c):
        each_x(c, lambda copy: copy.wait_send())

        @pl.when(lat < n_lat - 1)
        def _():
            halo_up(c).wait_send()

        @pl.when(lat > 0)
        def _():
            halo_down(c).wait_send()

        each_end(c, lambda copy: copy.wait_send())

    @pl.when(first < last)
    def _():
        pl.when(local)(prepare)
        if helping:

            @pl.when(tm == helped)
            def _():
                prm_copy().start()

            @pl.when(is_helper)
            def _():
                prm_copy().wait_recv()

        loop(0, rows, build)
        loop(first, last + 1, step)

    def subtract(place):
        moved = prev[place].astype(jnp.float32)
        result[place] = (mine[place].astype(jnp.float32) - moved).astype(result.dtype)

    @pl.when(tm > 0)
    def _():
        to_mine.wait()

        def collect(c):
            end_copy(c, False).wait_recv()
            subtract(pl.ds(c * CHUNK, CHUNK))

        loop(0, steps - 1, collect)
        end_copy(steps - 1, True).wait_recv()
        subtract(pl.ds((steps - 1) * CHUNK, rest))

    pl.when(tm == 0)(to_result.wait)
    loop(first, last, settle)
    if helping:

        @pl.when(tm == helped)
        def _():
            prm_copy().wait_send()
            loop(half, steps, lambda c: raw_copy(c).wait_send())


def body(sizes, state, band_counts, dep_blocks, lon_entry, lon_offset, lon_frac, lat_offset, lat_frac):
    fields_n, levels, rows, cols = state.shape[1:]
    depth, blocks = fields_n * levels, cols // BLK
    n_tm, n_lat, n_lon = sizes
    plan = source_plan(blocks, n_lon)
    _, pieces, n_src = plan
    steps = -(-depth // CHUNK)
    flat = state.reshape(depth, rows, cols)

    lists = jnp.transpose(dep_blocks, (0, 3, 2, 1))
    dma = pltpu.SemaphoreType.DMA
    n_pieces = len(pieces)
    misfit = pl.pallas_call(
        functools.partial(kernel, plan, steps, depth, sizes),
        out_shape=pltpu.VMEM(flat.shape, flat.dtype),
        in_specs=[pl.BlockSpec(memory_space=pltpu.HBM)] * 8,
        out_specs=pl.BlockSpec(memory_space=pltpu.VMEM),
        scratch_shapes=[
            pltpu.VMEM((steps, CHUNK, rows, cols), flat.dtype),
            *[pltpu.VMEM((steps, CHUNK, rows, p[2] * BLK), flat.dtype) for p in pieces],
            pltpu.VMEM(flat.shape, flat.dtype),
            pltpu.VMEM(flat.shape, flat.dtype),
            dma(()),
            pltpu.SMEM(band_counts.shape, jnp.int32),
            pltpu.SMEM(lists.shape, jnp.int32),
            *[
                pltpu.VMEM((rows, cols), kind.dtype)
                for kind in (lon_entry, lon_offset, lon_frac, lat_offset, lat_frac)
            ],
            pltpu.VMEM((n_src, CHUNK * rows, BLK), jnp.float32),
            pltpu.VMEM((11, rows, cols), jnp.float32),
            pltpu.VMEM((rows, n_src * BLK, cols), jnp.bfloat16),
            pltpu.VMEM((steps, rows + 4, CHUNK, cols), flat.dtype),
            pltpu.VMEM((blocks, CHUNK * rows, BLK), jnp.float32),
            pltpu.VMEM((steps, CHUNK, rows, cols), flat.dtype),
            dma((steps,)),
            dma((n_pieces, steps)),
            dma((n_pieces, steps)),
            dma((2, steps)),
            dma((2, steps)),
            dma((steps,)),
            dma((steps,)),
            dma((steps,)),
            dma(()),
            dma(()),
            dma((7,)),
        ],
        compiler_params=pltpu.CompilerParams(
            collective_id=0, has_side_effects=True, vmem_limit_bytes=60 * 1024 * 1024
        ),
    )(
        pltpu.with_memory_space_constraint(flat, pltpu.HBM),
        band_counts,
        *[
            pltpu.with_memory_space_constraint(array, pltpu.HBM)
            for array in (lists, lon_entry, lon_offset, lon_frac, lat_offset, lat_frac)
        ],
    )
    return misfit.reshape(state.shape)


def solution(mesh):
    placed = (
        P("tm", None, None, "lat", "lon"),
        P("tm", "lat"),
        P("tm", "lat", "lon", None),
        P("tm", "lat", "lon"),
        P("tm", "lat", "lon"),
        P("tm", "lat", "lon"),
        P("tm", "lat", "lon"),
        P("tm", "lat", "lon"),
    )
    sizes = tuple(mesh.shape[name] for name in ("tm", "lat", "lon"))
    return jax.shard_map(
        functools.partial(body, sizes),
        mesh=mesh,
        in_specs=placed,
        out_specs=P("tm", None, None, "lat", "lon"),
        check_vma=False,
    )
```
